32 devices in a mesh: mesh: 8 (over z, y), harm: 4 (over x, core).
Axes of the slice: x: 2, y: 2, z: 4, core: 2. Of those that a mesh axis runs over, the one named last changes fastest.
Arguments:
- displacement: float32 [32, 3, 16, 32, 256], P('harm', None, 'mesh'), may hold values from -3 to 3
- direction: float32 [32, 3, 16, 32, 256], P('harm', None, 'mesh'), may hold values from -6 to 6
- forcing: float32 [32, 3, 16, 32, 256], P('harm', None, 'mesh'), may hold values from -6 to 6
- stiffness: float32 [16, 32, 256], P('mesh'), may hold values from 0.5 to 3
- lumped_mass: float32 [16, 32, 256], P('mesh'), may hold values from 0.5 to 2
- face_cells: int32 [8192], P('mesh'), may hold values from 0 to 16383, as said below
- send_rows: int32 [8192], P('mesh'), may hold values from 0 to 1024, as said below
- pair_rows: int32 [2, 2048], P(None, 'mesh'), may hold values from 0 to 1023, as said below
- status: int32 [64, 2048], P('harm', 'mesh'), may hold values 0 or 1
- crack_gap: float32 [2048], P('mesh'), may hold values from -1 to 1
Outputs:
- residual: float32 [32, 3, 16, 32, 256], P('harm', None, 'mesh')
- jacobian_product: float32 [32, 3, 16, 32, 256], P('harm', None, 'mesh')
The draws below stay inside these ranges and needn't reach their ends.
Inputs may be any that keep to these rules, and one draw needn't show every extreme that they name: `face_cells`: each sector's 1024 entries are distinct cells of its block. `send_rows`: the crack crosses a contiguous arc of 4 sectors that passes over the cycle's seam (it holds sectors 8 - 1 and 0). Each sector of the arc sends every one of its 1024 face rows in exactly one slot, so each owner gets exactly 128 rows from each sector of the arc; the other sectors' slots all hold 1024, meaning empty. `pair_rows`: each owner's 2 * 256 entries are exactly the slots it receives from the sectors of the arc, each once.
All inputs are finite; a program needn't handle non-finite values. No bound on the sum of `status` on one device may be relied on, other than what follows from the above.
Results may differ from the reference program's by a relative error of at most 0.00005.
Values sent between devices are 32-bit elements; how exact they have to be, the bound alone decides.
No kernel may reach another device: no remote copies, remote signals or barrier semaphores. Data moves between devices by JAX's collectives and lax.ppermute only.
A program may use at most 192 MiB of HBM per device.

```python
import math
import jax
import jax.numpy as jnp
from jax import lax

HARM = 16
COEF = 32
TIME = 64
CIRC_DEV = 2
RAD = 32
AX = 256
PAIR_DEV = 256
FACE_DEV = 1024
CAP = 128
CIRC = 16
PAIRS = 2048
N_MESH = 8


def arc_first(key):
    return jax.random.randint(jax.random.fold_in(key, 11), (), N_MESH // 2 + 1, N_MESH)


def draw_face_cells(key, part):
    cell_count = CIRC_DEV * RAD * AX
    device_keys = jax.random.split(jax.random.fold_in(key, 12), N_MESH)

    def one_sector(subkey):
        first_key, second_key = jax.random.split(subkey)
        interior = jax.random.permutation(first_key, cell_count - 2)[:FACE_DEV - 2] + 1
        chosen = jnp.concatenate([jnp.array([0, cell_count - 1], jnp.int32), interior.astype(jnp.int32)])
        return jax.random.permutation(second_key, chosen)
    return jax.vmap(one_sector)(device_keys).reshape(-1).astype(jnp.int32)


def draw_send_rows(key, part):
    first_sector = arc_first(key)
    device_keys = jax.random.split(jax.random.fold_in(key, 13), N_MESH)
    shuffled = jax.vmap(lambda subkey: jax.random.permutation(subkey, FACE_DEV))(device_keys).astype(jnp.int32)
    device = jnp.arange(N_MESH, dtype=jnp.int32)
    in_arc = (device - first_sector) % N_MESH < N_MESH // 2
    return jnp.where(in_arc[:, None], shuffled, FACE_DEV).reshape(-1).astype(jnp.int32)


def draw_pair_rows(key, part):
    first_sector = arc_first(key)
    sources = (first_sector + jnp.arange(N_MESH // 2, dtype=jnp.int32)) % N_MESH
    positions = (sources[:, None] * CAP + jnp.arange(CAP, dtype=jnp.int32)[None, :]).reshape(-1)
    device_keys = jax.random.split(jax.random.fold_in(key, 14), N_MESH)
    shuffled = jax.vmap(lambda subkey: jax.random.permutation(subkey, positions))(device_keys)
    pair_table = shuffled.reshape(N_MESH, PAIR_DEV, 2)
    return jnp.transpose(pair_table, (2, 0, 1)).reshape(2, N_MESH * PAIR_DEV).astype(jnp.int32)


def with_ends(values, rng, low, top_value):
    dims = values.shape
    place = [jax.random.randint(jax.random.fold_in(rng, axis), (), 0, dims[axis]) for axis in range(len(dims))]
    values = values.at[tuple(place)].set(low)
    longest = dims.index(max(dims))
    place[longest] = (place[longest] + 1) % dims[longest]
    return values.at[tuple(place)].set(top_value)


def shard_levels(rng, dims, shards, least, largest):
    loudness = 1.0
    for axis_at, blocks in shards:
        steps = jax.random.uniform(jax.random.fold_in(jax.random.fold_in(rng, 6), axis_at), (blocks,), jnp.float32, least / len(shards), largest / len(shards))
        loudness = loudness * jnp.repeat(jnp.exp(steps), dims[axis_at] // blocks).reshape((-1,) + (1,) * (len(dims) - 1 - axis_at))
    return loudness


def bell_draw(stream_key, dims, width, limit, shards=(), kind=jnp.bfloat16):
    values = jax.random.normal(stream_key, dims, jnp.float32) * width
    if len(shards) > 0:
        values = shard_levels(stream_key, dims, shards, -0.22, 0.18) * values
    return jnp.clip(values, min=-limit, max=limit).astype(kind)


def setup_inputs(seed: int = 0) -> dict:
    key_list = jax.random.split(jax.random.key(seed), 11)
    displacement = bell_draw(key_list[0], (COEF, 3, CIRC, RAD, AX), 0.5, 3.0, ((0, 4), (2, 8)), jnp.float32)
    direction = bell_draw(key_list[1], (COEF, 3, CIRC, RAD, AX), 1.0, 6.0, ((0, 4), (2, 8)), jnp.float32)
    forcing = bell_draw(key_list[2], (COEF, 3, CIRC, RAD, AX), 1.0, 6.0, ((0, 4), (2, 8)), jnp.float32)
    stiffness = jnp.clip(0.5 + 2.5 * jax.random.uniform(key_list[3], (CIRC, RAD, AX), jnp.float32) ** shard_levels(key_list[3], (CIRC, RAD, AX), ((0, 8),), -0.2, 0.2), 0.5, 3.0)
    lumped_mass = jnp.clip(jnp.exp(math.log(2.0) - 1.3862944 * jax.random.uniform(key_list[4], (CIRC, RAD, AX), jnp.float32) ** shard_levels(key_list[4], (CIRC, RAD, AX), ((0, 8),), -0.2, 0.2)), 0.5, 2.0)
    face_cells = draw_face_cells(jax.random.fold_in(key_list[10], 71), 0)
    send_rows = draw_send_rows(jax.random.fold_in(key_list[10], 71), 0)
    pair_rows = draw_pair_rows(jax.random.fold_in(key_list[10], 71), 0)
    status = with_ends((jax.random.randint(key_list[8], (TIME, PAIRS), 0, 2) < 1).astype(jnp.int32), jax.random.fold_in(key_list[8], 1), 0, 1)
    crack_gap = jnp.clip(jax.random.uniform(key_list[9], (PAIRS,), jnp.float32, -1.0, 1.0) * shard_levels(key_list[9], (PAIRS,), ((0, 8),), -0.4, 0.0), -1.0, 1.0)
    return dict(displacement=displacement, direction=direction, forcing=forcing, stiffness=stiffness, lumped_mass=lumped_mass, face_cells=face_cells, send_rows=send_rows, pair_rows=pair_rows, status=status, crack_gap=crack_gap)


damping_ratio = 0.3
normal_penalty = 2.0
shear_penalty = 1.0


def transform_table(time_count, coef_count):
    sample_index = jnp.arange(time_count, dtype=jnp.int32)[:, None]
    coef_index = jnp.arange(coef_count, dtype=jnp.int32)[None, :]
    harmonic = coef_index // 2 + 1
    angles = ((harmonic * sample_index) % time_count).astype(jnp.float32) * (2.0 * math.pi / time_count)
    return jnp.where(coef_index % 2 == 0, jnp.cos(angles), jnp.sin(angles))


def reference(displacement, direction, forcing, stiffness, lumped_mass, face_cells, send_rows, pair_rows, status, crack_gap):
    fields = jnp.stack([displacement, direction])
    coef_total = fields.shape[1]
    neighbours = jnp.roll(fields, 1, axis=3) + jnp.roll(fields, -1, axis=3)
    rad_pad = jnp.pad(fields, ((0, 0), (0, 0), (0, 0), (0, 0), (1, 1), (0, 0)))
    neighbours = neighbours + rad_pad[:, :, :, :, 2:, :] + rad_pad[:, :, :, :, :-2, :]
    ax_pad = jnp.pad(fields, ((0, 0), (0, 0), (0, 0), (0, 0), (0, 0), (1, 1)))
    neighbours = neighbours + ax_pad[..., 2:] + ax_pad[..., :-2]
    stiff_part = (6.0 + stiffness) * fields - neighbours
    paired = fields.reshape((2, coef_total // 2, 2) + fields.shape[2:])
    turned = jnp.stack([paired[:, :, 1], -paired[:, :, 0]], axis=2).reshape(fields.shape)
    harmonic = jnp.arange(coef_total, dtype=jnp.int32) // 2 + 1
    frequency = (harmonic.astype(jnp.float32) * (1.5 / HARM))[None, :, None, None, None, None]
    linear = stiff_part - frequency * frequency * lumped_mass * fields + frequency * damping_ratio * lumped_mass * turned

    device = jnp.arange(N_MESH, dtype=jnp.int32)[:, None]
    local_cells = face_cells.reshape(N_MESH, FACE_DEV)
    block_cells = RAD * AX
    circ_index = device * CIRC_DEV + local_cells // block_cells
    flat_index = (circ_index * block_cells + local_cells % block_cells).reshape(-1).astype(jnp.int32)
    flat_fields = fields.reshape(2, coef_total, 3, -1)
    face_values = jnp.take(flat_fields, flat_index, axis=3)
    dft_table = transform_table(TIME, coef_total)
    samples = jnp.einsum("tc,ickf->tikf", dft_table, face_values, precision=lax.Precision.HIGHEST)

    send_table = send_rows.reshape(N_MESH, FACE_DEV)
    pair_table = pair_rows.reshape(2, N_MESH, PAIR_DEV)
    owners = jnp.arange(N_MESH, dtype=jnp.int32)[None, :, None]
    source = pair_table // CAP
    slot_index = pair_table % CAP
    local_row = send_table[source, owners * CAP + slot_index]
    global_row = (source * FACE_DEV + local_row).reshape(2, -1).astype(jnp.int32)
    side_a = jnp.take(samples, global_row[0], axis=3)
    side_b = jnp.take(samples, global_row[1], axis=3)
    opening = side_a - side_b
    opening = opening.at[:, 0, 0, :].add(crack_gap[None, :])
    penalty = jnp.array([normal_penalty, shear_penalty, shear_penalty], jnp.float32)[None, None, :, None]
    closed = status.astype(jnp.float32)[:, None, None, :]
    pair_force = closed * penalty * opening
    on_rows = jnp.zeros_like(samples).at[..., global_row[0]].add(pair_force).at[..., global_row[1]].add(-pair_force)
    coef_force = (2.0 / TIME) * jnp.einsum("tc,tikf->cikf", dft_table, on_rows, precision=lax.Precision.HIGHEST)
    contact = jnp.zeros_like(flat_fields).at[..., flat_index].add(jnp.transpose(coef_force, (1, 0, 2, 3)))
    combined = linear + contact.reshape(fields.shape)
    return combined[0] - forcing, combined[1]
```

```python
import math

import jax
import jax.numpy as jnp
import numpy as np
from jax import lax
from jax.experimental import pallas as pl
from jax.experimental.pallas import tpu as pltpu
from jax.sharding import PartitionSpec as P

HARM = 16
TIME = 64
LANES = 128

damping_ratio = 0.3
normal_penalty = 2.0
shear_penalty = 1.0

CHUNKS = ((0, 1), (1, 4), (4, 7), (7, 8))
VMEM = 56 * 1024 * 1024


def split2(value):
    high = value.astype(jnp.bfloat16)
    low = (value - high.astype(jnp.float32)).astype(jnp.bfloat16)
    return high, low


def split3(value):
    high = value.astype(jnp.bfloat16)
    rest = value - high.astype(jnp.float32)
    mid = rest.astype(jnp.bfloat16)
    low = (rest - mid.astype(jnp.float32)).astype(jnp.bfloat16)
    return high, mid, low


def slot_cells(cells_ref, send_ref):
    rows = cells_ref.shape[0]
    send = send_ref[...]
    high = send // LANES
    low = send % LANES
    found = jnp.zeros_like(send)
    for row in range(rows):
        table = jnp.broadcast_to(cells_ref[row : row + 1, :], send.shape)
        picked = jnp.take_along_axis(table, low, axis=1)
        found = jnp.where(high == row, picked, found)
    return jnp.concatenate([found[row : row + 1, :] for row in range(rows)], axis=1)


def one_hot_rows(index_row, count, kind):
    shape = (count, index_row.shape[1])
    hit = lax.broadcasted_iota(jnp.int32, shape, 0) == index_row
    return jnp.where(hit, 1.0, 0.0).astype(kind)


def gather_kernel(cells_ref, send_ref, x_ref, y_ref, out_ref, cell_ref, low_ref):
    comp = pl.program_id(0)
    coefs, _, rows, axial = x_ref.shape
    slots = cell_ref.shape[1]

    @pl.when(comp == 0)
    def _():
        cell = slot_cells(cells_ref, send_ref)
        cell_ref[...] = cell
        hot = one_hot_rows(cell % axial, axial, jnp.bfloat16)
        low_ref[0:axial, :] = hot
        low_ref[axial : 2 * axial, :] = hot

    row_of = cell_ref[...] // axial
    mask = lax.broadcasted_iota(jnp.int32, (rows, slots), 0) == row_of
    for field, ref in enumerate((x_ref, y_ref)):
        flat = ref[...].reshape(coefs * rows, axial)
        high, low = split2(flat)
        picked = jnp.dot(
            jnp.concatenate([high, low], axis=1),
            low_ref[...],
            preferred_element_type=jnp.float32,
        ).reshape(coefs, rows, slots)
        values = jnp.sum(jnp.where(mask[None], picked, 0.0), axis=1)
        block = field * 3 + comp
        if len(out_ref.shape) == 4:
            cap = out_ref.shape[3]
            for owner in range(out_ref.shape[0]):
                out_ref[owner, block] = values[:, owner * cap : (owner + 1) * cap]
        else:
            out_ref[block] = values


def pair_table(pairs_ref, slots):
    count = pairs_ref.shape[1]
    place = lax.broadcasted_iota(jnp.int32, (slots, count), 0)
    side_a = jnp.where(place == pairs_ref[0:1, :], 1.0, 0.0)
    side_b = jnp.where(place == pairs_ref[1:2, :], 1.0, 0.0)
    return (side_a - side_b).astype(jnp.bfloat16)


def by_slot(ref, block):
    if len(ref.shape) == 3:
        return ref[block]
    return jnp.concatenate([ref[owner, block] for owner in range(ref.shape[0])], axis=1)


def opening_kernel(pairs_ref, status_ref, arrived_ref, out_ref):
    arrived = jnp.concatenate([by_slot(arrived_ref, block) for block in range(6)], axis=0)
    values, slots = arrived.shape
    table = pair_table(pairs_ref, slots)
    total = None
    for part in split3(arrived):
        term = jnp.dot(part, table, preferred_element_type=jnp.float32)
        total = term if total is None else total + term
    out_ref[0:values, :] = total
    out_ref[values:, :] = status_ref[...].astype(jnp.float32)


def force_kernel(place_ref, pairs_ref, gap_ref, table_ref, back_ref, all_ref, out_ref):
    harm_count, total_rows, pairs = all_ref.shape
    coefs = table_ref.shape[1] // harm_count
    values = 6 * coefs
    back = back_ref[place_ref[0]]
    closed = jnp.concatenate([all_ref[g, values:total_rows, :] for g in range(harm_count)], axis=0)
    coef_rows = []
    for block in range(6):
        spread = jnp.concatenate(
            [all_ref[g, block * coefs : (block + 1) * coefs, :] for g in range(harm_count)], axis=0
        )
        opening = jnp.dot(
            table_ref[...], spread, precision=lax.Precision.HIGHEST, preferred_element_type=jnp.float32
        )
        if block == 0:
            opening = opening + gap_ref[...]
        kappa = normal_penalty if block % 3 == 0 else shear_penalty
        force = closed * kappa * opening
        coef_rows.append(
            jnp.dot(back, force, precision=lax.Precision.HIGHEST, preferred_element_type=jnp.float32)
        )
    coef_force = jnp.concatenate(coef_rows, axis=0)
    direct = len(out_ref.shape) == 4
    slots = out_ref.shape[0] * out_ref.shape[3] if direct else out_ref.shape[2]
    table = pair_table(pairs_ref, slots)
    total = None
    for part in split3(coef_force):
        term = lax.dot_general(
            part, table, (((1,), (1,)), ((), ())), preferred_element_type=jnp.float32
        )
        total = term if total is None else total + term
    for block in range(6):
        part = total[block * coefs : (block + 1) * coefs]
        if direct:
            cap = out_ref.shape[3]
            for owner in range(out_ref.shape[0]):
                out_ref[owner, block] = part[:, owner * cap : (owner + 1) * cap]
        else:
            out_ref[block] = part


def local_kernel(place_ref, stiff_ref, mass_ref, x_ref, y_ref, forcing_ref, res_ref, jac_ref):
    _, comps, rows, axial = x_ref.shape
    layer = rows // 2
    harmonic = place_ref[0] * pl.num_programs(0) + pl.program_id(0) + 1
    frequency = harmonic.astype(jnp.float32) * (1.5 / HARM)
    mass = mass_ref[...]
    diagonal = 6.0 + stiff_ref[...] - (frequency * frequency) * mass
    turn = (frequency * damping_ratio) * mass
    row = lax.broadcasted_iota(jnp.int32, (rows, axial), 0) % layer
    column = lax.broadcasted_iota(jnp.int32, (rows, axial), 1)
    for ref, out_ref, forced in ((x_ref, res_ref, True), (y_ref, jac_ref, False)):
        for comp in range(comps):
            cosine = ref[0, comp]
            sine = ref[1, comp]
            for part, value, turned in ((0, cosine, sine), (1, sine, -cosine)):
                near = jnp.where(row == 0, 0.0, jnp.roll(value, 1, axis=0))
                near = near + jnp.where(row == layer - 1, 0.0, jnp.roll(value, -1, axis=0))
                near = near + jnp.where(column == 0, 0.0, pltpu.roll(value, 1, axis=1))
                near = near + jnp.where(column == axial - 1, 0.0, pltpu.roll(value, axial - 1, axis=1))
                near = near + jnp.concatenate([value[layer:], value[:layer]], axis=0)
                result = diagonal * value + turn * turned - near
                if forced:
                    result = result - forcing_ref[part, comp]
                out_ref[part, comp] = result


def scatter_kernel(cells_ref, send_ref, back_ref, *refs, spans):
    count = len(spans)
    halos = refs[: 4 * count]
    res_in, jac_in, res_ref, jac_ref, cell_ref, low_ref = refs[4 * count :]
    comp = pl.program_id(0)
    coefs, _, rows, axial = res_ref.shape
    slots = cell_ref.shape[1]
    layer = rows // 2

    @pl.when(comp == 0)
    def _():
        cell = slot_cells(cells_ref, send_ref)
        cell_ref[...] = cell
        low_ref[...] = one_hot_rows(cell % axial, axial, jnp.bfloat16)

    row_of = cell_ref[...] // axial
    mask = lax.broadcasted_iota(jnp.int32, (rows, slots), 0) == row_of
    for field, (in_ref, out_ref) in enumerate(((res_in, res_ref), (jac_in, jac_ref))):
        force = by_slot(back_ref, field * 3 + comp)
        total = None
        for part in split2(force):
            wide = part.astype(jnp.float32)
            spread = jnp.where(mask[None], wide[:, None, :], 0.0).astype(jnp.bfloat16)
            term = lax.dot_general(
                spread.reshape(coefs * rows, slots),
                low_ref[...],
                (((1,), (1,)), ((), ())),
                preferred_element_type=jnp.float32,
            )
            total = term if total is None else total + term
        total = in_ref[...].reshape(coefs, rows, axial) + total.reshape(coefs, rows, axial)
        out_ref[...] = total.reshape(coefs, 1, rows, axial)
        for index, (first, last) in enumerate(spans):
            below, above = halos[4 * index + 2 * field : 4 * index + 2 * field + 2]
            out_ref[first:last, 0, 0:layer, :] = total[first:last, 0:layer] - below[:, 0]
            out_ref[first:last, 0, layer:rows, :] = total[first:last, layer:rows] - above[:, 0]


def tail_kernel(res_in, jac_in, *refs):
    res_ref, jac_ref = refs[-2:]
    layer = res_ref.shape[2] // 2
    for field, (in_ref, out_ref) in enumerate(((res_in, res_ref), (jac_in, jac_ref))):
        below, above = refs[2 * field : 2 * field + 2]
        out_ref[:, :, 0:layer, :] = in_ref[:, :, 0:layer, :] - below[...]
        out_ref[:, :, layer:, :] = in_ref[:, :, layer:, :] - above[...]


def transform_table(time_count, coef_count):
    sample = np.arange(time_count)[:, None]
    coef = np.arange(coef_count)[None, :]
    angles = ((coef // 2 + 1) * sample % time_count) * (2.0 * math.pi / time_count)
    return np.where(coef % 2 == 0, np.cos(angles), np.sin(angles)).astype(np.float32)


def params(*semantics):
    return pltpu.CompilerParams(vmem_limit_bytes=VMEM, dimension_semantics=semantics or None)


def on_device(
    displacement,
    direction,
    forcing,
    stiffness,
    lumped_mass,
    face_cells,
    send_rows,
    pair_rows,
    status,
    crack_gap,
):
    coefs, comps, layers, radial, axial = displacement.shape
    rows = layers * radial
    slots = face_cells.shape[0]
    pairs = pair_rows.shape[1]
    owners = lax.axis_size("mesh")
    cap = slots // owners
    direct = cap % LANES == 0
    harm_count = lax.axis_size("harm")
    harm_index = lax.axis_index("harm")
    coef_total = coefs * harm_count
    place = jnp.reshape(harm_index, (1,)).astype(jnp.int32)
    f32 = jnp.float32
    values = 2 * comps * coefs
    wire = (owners, 6, coefs, cap) if direct else (6, coefs, slots)

    forward = [(i, (i + 1) % owners) for i in range(owners)]
    backward = [(target, source) for source, target in forward]

    def halo(first, last):
        pieces = []
        for field in (displacement, direction):
            part = field[first:last]
            pieces.append(lax.ppermute(part[:, :, layers - 1], "mesh", forward))
            pieces.append(lax.ppermute(part[:, :, 0], "mesh", backward))
        return pieces

    ends = sorted({a * coefs // 8 for span in CHUNKS for a in span})
    spans = list(zip(ends[:-1], ends[1:]))
    pieces = [halo(*span) for span in spans]

    x = displacement.reshape(coefs, comps, rows, axial)
    y = direction.reshape(coefs, comps, rows, axial)
    cells = face_cells.reshape(slots // LANES, LANES)
    send = send_rows.reshape(slots // LANES, LANES)
    whole = lambda shape: pl.BlockSpec(shape, lambda *_: (0,) * len(shape))
    scalar = pl.BlockSpec(memory_space=pltpu.SMEM)
    per_comp = pl.BlockSpec((coefs, 1, rows, axial), lambda comp: (0, comp, 0, 0))

    outgoing = pl.pallas_call(
        gather_kernel,
        grid=(comps,),
        in_specs=[whole(cells.shape), whole(send.shape), per_comp, per_comp],
        out_specs=whole(wire),
        out_shape=jax.ShapeDtypeStruct(wire, f32),
        scratch_shapes=[
            pltpu.VMEM((1, slots), jnp.int32),
            pltpu.VMEM((2 * axial, slots), jnp.bfloat16),
        ],
        compiler_params=params("arbitrary"),
        name="face_gather",
    )(cells, send, x, y)

    def exchange(block):
        if not direct:
            block = block.reshape(values, owners, cap).transpose(1, 0, 2)
        block = lax.all_to_all(block, "mesh", split_axis=0, concat_axis=0, tiled=True)
        if not direct:
            block = block.transpose(1, 0, 2).reshape(wire)
        return block

    arrived = exchange(outgoing)
    own_opening = pl.pallas_call(
        opening_kernel,
        in_specs=[whole(pair_rows.shape), whole(status.shape), whole(wire)],
        out_specs=whole((values + status.shape[0], pairs)),
        out_shape=jax.ShapeDtypeStruct((values + status.shape[0], pairs), f32),
        compiler_params=params(),
        name="pair_difference",
    )(pair_rows, status, arrived)
    everything = lax.all_gather(own_opening, "harm")
    table = transform_table(TIME, coef_total)
    back = ((2.0 / TIME) * table.T).reshape(harm_count, coefs, TIME)
    slot_force = pl.pallas_call(
        force_kernel,
        in_specs=[
            scalar,
            whole(pair_rows.shape),
            whole((1, pairs)),
            whole(table.shape),
            whole(back.shape),
            whole(everything.shape),
        ],
        out_specs=whole(wire),
        out_shape=jax.ShapeDtypeStruct(wire, f32),
        compiler_params=params(),
        name="pair_force",
    )(place, pair_rows, crack_gap.reshape(1, pairs), jnp.asarray(table), jnp.asarray(back), everything)
    returned = exchange(slot_force)

    per_harmonic = pl.BlockSpec((2, comps, rows, axial), lambda i: (i, 0, 0, 0))
    flat = jax.ShapeDtypeStruct(x.shape, f32)
    residual, product = pl.pallas_call(
        local_kernel,
        grid=(coefs // 2,),
        in_specs=[scalar, whole((rows, axial)), whole((rows, axial))] + [per_harmonic] * 3,
        out_specs=[per_harmonic] * 2,
        out_shape=[flat, flat],
        compiler_params=params("arbitrary"),
        name="local_terms",
    )(
        place,
        stiffness.reshape(rows, axial),
        lumped_mass.reshape(rows, axial),
        x,
        y,
        forcing.reshape(x.shape),
    )

    early, late = (spans[:-2], spans[-2:])
    near = [piece for chunk in pieces[: len(early)] for piece in chunk]
    near_specs = [
        pl.BlockSpec((last - first, 1, radial, axial), lambda comp: (0, comp, 0, 0))
        for first, last in early
        for _ in range(4)
    ]
    fixed = 3 + len(near)
    residual, product = pl.pallas_call(
        lambda *refs: scatter_kernel(*refs, spans=early),
        grid=(comps,),
        in_specs=[whole(cells.shape), whole(send.shape), whole(wire)] + near_specs + [per_comp] * 2,
        out_specs=[per_comp] * 2,
        out_shape=[flat, flat],
        input_output_aliases={fixed: 0, fixed + 1: 1},
        scratch_shapes=[
            pltpu.VMEM((1, slots), jnp.int32),
            pltpu.VMEM((axial, slots), jnp.bfloat16),
        ],
        compiler_params=params("arbitrary"),
        name="face_scatter",
    )(cells, send, returned, *near, residual, product)

    for (first, last), chunk in zip(late, pieces[len(early) :]):
        mine = pl.BlockSpec((1, comps, rows, axial), lambda i, first=first: (first + i, 0, 0, 0))
        edge = pl.BlockSpec((1, comps, radial, axial), lambda i: (i, 0, 0, 0))
        residual, product = pl.pallas_call(
            tail_kernel,
            grid=(last - first,),
            in_specs=[mine] * 2 + [edge] * 4,
            out_specs=[mine] * 2,
            out_shape=[flat, flat],
            input_output_aliases={0: 0, 1: 1},
            compiler_params=params("arbitrary"),
            name="edge_terms",
        )(residual, product, *chunk)
    return residual.reshape(displacement.shape), product.reshape(displacement.shape)


def solution(mesh):
    placed = (
        P("harm", None, "mesh", None, None),
        P("harm", None, "mesh", None, None),
        P("harm", None, "mesh", None, None),
        P("mesh", None, None),
        P("mesh", None, None),
        P("mesh"),
        P("mesh"),
        P(None, "mesh"),
        P("harm", "mesh"),
        P("mesh"),
    )
    return jax.shard_map(
        on_device,
        mesh=mesh,
        in_specs=placed,
        out_specs=(P("harm", None, "mesh", None, None), P("harm", None, "mesh", None, None)),
        check_vma=False,
    )
```

```python
import math

import jax
import jax.numpy as jnp
import numpy as np
from jax import lax
from jax.experimental import pallas as pl
from jax.experimental.pallas import tpu as pltpu
from jax.sharding import PartitionSpec as P

HARM = 16
TIME = 64
LANES = 128

damping_ratio = 0.3
normal_penalty = 2.0
shear_penalty = 1.0

CUTS = (0, 3, 7, 8)
VMEM = 28 * 1024 * 1024


def split2(value):
    high = value.astype(jnp.bfloat16)
    low = (value - high.astype(jnp.float32)).astype(jnp.bfloat16)
    return high, low


def split3(value):
    high = value.astype(jnp.bfloat16)
    rest = value - high.astype(jnp.float32)
    mid = rest.astype(jnp.bfloat16)
    low = (rest - mid.astype(jnp.float32)).astype(jnp.bfloat16)
    return high, mid, low


def slot_cells(cells_ref, send_ref):
    rows = cells_ref.shape[0]
    send = send_ref[...]
    high = send // LANES
    low = send % LANES
    found = jnp.zeros_like(send)
    for row in range(rows):
        table = jnp.broadcast_to(cells_ref[row : row + 1, :], send.shape)
        picked = jnp.take_along_axis(table, low, axis=1)
        found = jnp.where(high == row, picked, found)
    return jnp.concatenate([found[row : row + 1, :] for row in range(rows)], axis=1)


def one_hot_rows(index_row, count, kind):
    shape = (count, index_row.shape[1])
    hit = lax.broadcasted_iota(jnp.int32, shape, 0) == index_row
    return jnp.where(hit, 1.0, 0.0).astype(kind)


def gather_kernel(cells_ref, send_ref, x_ref, y_ref, out_ref, *refs, edges):
    edge_refs = refs[: len(edges)]
    cell_ref, low_ref = refs[len(edges) :]
    comp = pl.program_id(0)
    coefs, _, rows, axial = x_ref.shape
    slots = cell_ref.shape[1]

    @pl.when(comp == 0)
    def _():
        cell = slot_cells(cells_ref, send_ref)
        cell_ref[...] = cell
        hot = one_hot_rows(cell % axial, axial, jnp.bfloat16)
        low_ref[0:axial, :] = hot
        low_ref[axial : 2 * axial, :] = hot

    row_of = cell_ref[...] // axial
    mask = lax.broadcasted_iota(jnp.int32, (rows, slots), 0) == row_of
    for field, ref in enumerate((x_ref, y_ref)):
        for edge_ref, (start, first, last) in zip(edge_refs, edges):
            edge_ref[field, :, 0] = ref[first:last, 0, start : start + rows // 2]
        flat = ref[...].reshape(coefs * rows, axial)
        high, low = split2(flat)
        picked = jnp.dot(
            jnp.concatenate([high, low], axis=1),
            low_ref[...],
            preferred_element_type=jnp.float32,
        ).reshape(coefs, rows, slots)
        values = jnp.sum(jnp.where(mask[None], picked, 0.0), axis=1)
        block = field * 3 + comp
        if len(out_ref.shape) == 4:
            cap = out_ref.shape[3]
            for owner in range(out_ref.shape[0]):
                out_ref[owner, block] = values[:, owner * cap : (owner + 1) * cap]
        else:
            out_ref[block] = values


def pair_table(pairs_ref, slots):
    count = pairs_ref.shape[1]
    place = lax.broadcasted_iota(jnp.int32, (slots, count), 0)
    side_a = jnp.where(place == pairs_ref[0:1, :], 1.0, 0.0)
    side_b = jnp.where(place == pairs_ref[1:2, :], 1.0, 0.0)
    return (side_a - side_b).astype(jnp.bfloat16)


def by_slot(ref, block):
    if len(ref.shape) == 3:
        return ref[block]
    return jnp.concatenate([ref[owner, block] for owner in range(ref.shape[0])], axis=1)


def mark_kernel(piece_ref, out_ref):
    del piece_ref
    out_ref[...] = jnp.zeros_like(out_ref)


def opening_kernel(pairs_ref, status_ref, mark_ref, arrived_ref, out_ref):
    del mark_ref
    arrived = jnp.concatenate([by_slot(arrived_ref, block) for block in range(6)], axis=0)
    values, slots = arrived.shape
    table = pair_table(pairs_ref, slots)
    total = None
    for part in split3(arrived):
        term = jnp.dot(part, table, preferred_element_type=jnp.float32)
        total = term if total is None else total + term
    out_ref[0:values, :] = total
    out_ref[values:, :] = status_ref[...].astype(jnp.float32)


def force_kernel(place_ref, pairs_ref, gap_ref, table_ref, back_ref, all_ref, out_ref):
    harm_count, total_rows, pairs = all_ref.shape
    coefs = table_ref.shape[1] // harm_count
    values = 6 * coefs
    back = back_ref[place_ref[0]]
    closed = jnp.concatenate([all_ref[g, values:total_rows, :] for g in range(harm_count)], axis=0)
    coef_rows = []
    for block in range(6):
        spread = jnp.concatenate(
            [all_ref[g, block * coefs : (block + 1) * coefs, :] for g in range(harm_count)], axis=0
        )
        opening = jnp.dot(
            table_ref[...], spread, precision=lax.Precision.HIGHEST, preferred_element_type=jnp.float32
        )
        if block == 0:
            opening = opening + gap_ref[...]
        kappa = normal_penalty if block % 3 == 0 else shear_penalty
        force = closed * kappa * opening
        coef_rows.append(
            jnp.dot(back, force, precision=lax.Precision.HIGHEST, preferred_element_type=jnp.float32)
        )
    coef_force = jnp.concatenate(coef_rows, axis=0)
    direct = len(out_ref.shape) == 4
    slots = out_ref.shape[0] * out_ref.shape[3] if direct else out_ref.shape[2]
    table = pair_table(pairs_ref, slots)
    total = None
    for part in split3(coef_force):
        term = lax.dot_general(
            part, table, (((1,), (1,)), ((), ())), preferred_element_type=jnp.float32
        )
        total = term if total is None else total + term
    for block in range(6):
        part = total[block * coefs : (block + 1) * coefs]
        if direct:
            cap = out_ref.shape[3]
            for owner in range(out_ref.shape[0]):
                out_ref[owner, block] = part[:, owner * cap : (owner + 1) * cap]
        else:
            out_ref[block] = part


def combine_kernel(
    place_ref,
    cells_ref,
    send_ref,
    back_ref,
    below_ref,
    above_ref,
    stiff_ref,
    mass_ref,
    x_ref,
    y_ref,
    forcing_ref,
    res_ref,
    jac_ref,
    late_res_ref,
    late_jac_ref,
    cell_ref,
    low_ref,
):
    comp = pl.program_id(0)
    coefs, _, rows, axial = x_ref.shape
    slots = cell_ref.shape[1]
    layer = rows // 2
    early = below_ref.shape[1]

    @pl.when(comp == 0)
    def _():
        cell = slot_cells(cells_ref, send_ref)
        cell_ref[...] = cell
        low_ref[...] = one_hot_rows(cell % axial, axial, jnp.bfloat16)

    row_of = cell_ref[...] // axial
    mask = lax.broadcasted_iota(jnp.int32, (rows, slots), 0) == row_of
    row = lax.broadcasted_iota(jnp.int32, (rows, axial), 0) % layer
    column = lax.broadcasted_iota(jnp.int32, (rows, axial), 1)
    mass = mass_ref[...]
    stiff = 6.0 + stiff_ref[...]
    for field, (ref, out_ref, late_ref) in enumerate(
        ((x_ref, res_ref, late_res_ref), (y_ref, jac_ref, late_jac_ref))
    ):
        force = by_slot(back_ref, field * 3 + comp)
        contact = None
        for part in split2(force):
            wide = part.astype(jnp.float32)
            spread = jnp.where(mask[None], wide[:, None, :], 0.0).astype(jnp.bfloat16)
            term = lax.dot_general(
                spread.reshape(coefs * rows, slots),
                low_ref[...],
                (((1,), (1,)), ((), ())),
                preferred_element_type=jnp.float32,
            )
            contact = term if contact is None else contact + term
        contact = contact.reshape(coefs, rows, axial)
        for coef in range(coefs):
            harmonic = place_ref[0] * (coefs // 2) + (coef // 2 + 1)
            frequency = harmonic.astype(jnp.float32) * (1.5 / HARM)
            value = ref[coef, 0]
            turned = ref[coef + 1, 0] if coef % 2 == 0 else -ref[coef - 1, 0]
            near = jnp.where(row == 0, 0.0, jnp.roll(value, 1, axis=0))
            near = near + jnp.where(row == layer - 1, 0.0, jnp.roll(value, -1, axis=0))
            near = near + jnp.where(column == 0, 0.0, pltpu.roll(value, 1, axis=1))
            near = near + jnp.where(column == axial - 1, 0.0, pltpu.roll(value, axial - 1, axis=1))
            near = near + jnp.concatenate([value[layer:], value[:layer]], axis=0)
            result = (stiff - (frequency * frequency) * mass) * value - near
            result = result + (frequency * damping_ratio) * mass * turned + contact[coef]
            if field == 0:
                result = result - forcing_ref[coef, 0]
            if coef < early:
                out_ref[coef, 0, :layer] = result[:layer] - below_ref[field, coef, comp]
                out_ref[coef, 0, layer:] = result[layer:] - above_ref[field, coef, comp]
            else:
                late_ref[coef - early, comp] = result


def edge_kernel(late_res, late_jac, below, above, res_in, jac_in, res_ref, jac_ref, *, offset):
    del res_in, jac_in
    layer = res_ref.shape[2] // 2
    step = pl.program_id(0)
    for field, (late_ref, out_ref) in enumerate(((late_res, res_ref), (late_jac, jac_ref))):
        value = late_ref[offset + step]
        out_ref[0, :, :layer, :] = value[:, :layer] - below[field, step]
        out_ref[0, :, layer:, :] = value[:, layer:] - above[field, step]


def transform_table(time_count, coef_count):
    sample = np.arange(time_count)[:, None]
    coef = np.arange(coef_count)[None, :]
    angles = ((coef // 2 + 1) * sample % time_count) * (2.0 * math.pi / time_count)
    return np.where(coef % 2 == 0, np.cos(angles), np.sin(angles)).astype(np.float32)


SMALL = pl.CostEstimate(flops=1000, transcendentals=0, bytes_accessed=1000)
LARGE = pl.CostEstimate(flops=10**12, transcendentals=10**9, bytes_accessed=10**10)


def params(*semantics):
    return pltpu.CompilerParams(vmem_limit_bytes=VMEM, dimension_semantics=semantics or None)


def on_device(
    displacement,
    direction,
    forcing,
    stiffness,
    lumped_mass,
    face_cells,
    send_rows,
    pair_rows,
    status,
    crack_gap,
):
    coefs, comps, layers, radial, axial = displacement.shape
    rows = layers * radial
    slots = face_cells.shape[0]
    pairs = pair_rows.shape[1]
    owners = lax.axis_size("mesh")
    cap = slots // owners
    direct = cap % LANES == 0
    harm_count = lax.axis_size("harm")
    harm_index = lax.axis_index("harm")
    coef_total = coefs * harm_count
    place = jnp.reshape(harm_index, (1,)).astype(jnp.int32)
    f32 = jnp.float32
    values = 2 * comps * coefs
    wire = (owners, 6, coefs, cap) if direct else (6, coefs, slots)

    forward = [(i, (i + 1) % owners) for i in range(owners)]
    backward = [(target, source) for source, target in forward]
    ahead = lambda piece: lax.ppermute(piece, "mesh", forward)
    behind = lambda piece: lax.ppermute(piece, "mesh", backward)
    keep = lambda value: pltpu.with_memory_space_constraint(value, pltpu.VMEM)

    ends = [cut * coefs // 8 for cut in CUTS]
    spans = list(zip(ends[:-1], ends[1:]))
    early = ends[1]
    first_piece = jnp.stack([field[:early, :, layers - 1] for field in (displacement, direction)])
    below = [ahead(first_piece)]
    above = []

    x = displacement.reshape(coefs, comps, rows, axial)
    y = direction.reshape(coefs, comps, rows, axial)
    cells = face_cells.reshape(slots // LANES, LANES)
    send = send_rows.reshape(slots // LANES, LANES)
    whole = lambda shape: pl.BlockSpec(shape, lambda *_: (0,) * len(shape))
    scalar = pl.BlockSpec(memory_space=pltpu.SMEM)
    near_memory = pl.BlockSpec(memory_space=pltpu.VMEM)
    per_comp = pl.BlockSpec((coefs, 1, rows, axial), lambda comp: (0, comp, 0, 0))

    edges = [(0, 0, early)]
    edges += [(start, first, last) for first, last in spans[1:] for start in (radial, 0)]
    edge_shapes = [(2, last - first, comps, radial, axial) for _, first, last in edges]
    outgoing, *sent = pl.pallas_call(
        lambda *refs: gather_kernel(*refs, edges=edges),
        grid=(comps,),
        in_specs=[whole(cells.shape), whole(send.shape), per_comp, per_comp],
        out_specs=[whole(wire)]
        + [
            pl.BlockSpec(shape[:2] + (1,) + shape[3:], lambda comp: (0, 0, comp, 0, 0))
            for shape in edge_shapes
        ],
        out_shape=[jax.ShapeDtypeStruct(shape, f32) for shape in [wire] + edge_shapes],
        scratch_shapes=[
            pltpu.VMEM((1, slots), jnp.int32),
            pltpu.VMEM((2 * axial, slots), jnp.bfloat16),
        ],
        compiler_params=params("arbitrary"),
        cost_estimate=SMALL,
        name="face_gather",
    )(cells, send, x, y)

    def exchange(block):
        if not direct:
            block = block.reshape(values, owners, cap).transpose(1, 0, 2)
        block = lax.all_to_all(block, "mesh", split_axis=0, concat_axis=0, tiled=True)
        if not direct:
            block = block.transpose(1, 0, 2).reshape(wire)
        return block

    outgoing, sent[0] = lax.optimization_barrier((outgoing, sent[0]))
    mark = pl.pallas_call(
        mark_kernel,
        in_specs=[near_memory],
        out_specs=near_memory,
        out_shape=pltpu.VMEM((8, LANES), f32),
        cost_estimate=LARGE,
        name="first_piece_arrived",
    )(keep(below[0]))
    above.append(behind(sent[0]))
    arrived = exchange(outgoing)
    own_opening = pl.pallas_call(
        opening_kernel,
        in_specs=[whole(pair_rows.shape), whole(status.shape), near_memory, near_memory],
        out_specs=whole((values + status.shape[0], pairs)),
        out_shape=jax.ShapeDtypeStruct((values + status.shape[0], pairs), f32),
        compiler_params=params(),
        cost_estimate=SMALL,
        name="pair_difference",
    )(pair_rows, status, keep(mark), pltpu.with_memory_space_constraint(arrived, pltpu.VMEM))
    everything = lax.all_gather(own_opening, "harm")
    table = transform_table(TIME, coef_total)
    back = ((2.0 / TIME) * table.T).reshape(harm_count, coefs, TIME)
    slot_force = pl.pallas_call(
        force_kernel,
        in_specs=[
            scalar,
            whole(pair_rows.shape),
            whole((1, pairs)),
            whole(table.shape),
            whole(back.shape),
            whole(everything.shape),
        ],
        out_specs=whole(wire),
        out_shape=jax.ShapeDtypeStruct(wire, f32),
        compiler_params=params(),
        cost_estimate=LARGE,
        name="pair_force",
    )(place, pair_rows, crack_gap.reshape(1, pairs), jnp.asarray(table), jnp.asarray(back), everything)
    returned = exchange(slot_force)
    above[0], sent[1:], _ = lax.optimization_barrier((above[0], sent[1:], slot_force))
    below.append(ahead(sent[1]))
    above.append(behind(sent[2]))

    flat = jax.ShapeDtypeStruct(x.shape, f32)
    late_shape = pltpu.VMEM((coefs - early, comps, rows, axial), f32)
    residual, product, late_res, late_jac = pl.pallas_call(
        combine_kernel,
        grid=(comps,),
        in_specs=[scalar, whole(cells.shape), whole(send.shape)]
        + [near_memory] * 3
        + [whole((rows, axial))] * 2
        + [per_comp] * 3,
        out_specs=[per_comp] * 2 + [near_memory] * 2,
        out_shape=[flat, flat, late_shape, late_shape],
        scratch_shapes=[
            pltpu.VMEM((1, slots), jnp.int32),
            pltpu.VMEM((axial, slots), jnp.bfloat16),
        ],
        compiler_params=params("arbitrary"),
        cost_estimate=LARGE,
        name="combine_terms",
    )(
        place,
        cells,
        send,
        keep(returned),
        keep(below[0]),
        keep(above[0]),
        stiffness.reshape(rows, axial),
        lumped_mass.reshape(rows, axial),
        x,
        y,
        forcing.reshape(x.shape),
    )
    residual, sent[3:] = lax.optimization_barrier((residual, sent[3:]))
    below.append(ahead(sent[3]))
    above.append(behind(sent[4]))

    for (first, last), low_edge, high_edge in zip(spans[1:], below[1:], above[1:]):
        mine = pl.BlockSpec((1, comps, rows, axial), lambda i, first=first: (first + i, 0, 0, 0))
        residual, product = pl.pallas_call(
            lambda *refs, offset=first - early: edge_kernel(*refs, offset=offset),
            grid=(last - first,),
            in_specs=[near_memory] * 4 + [pl.BlockSpec(memory_space=pl.ANY)] * 2,
            out_specs=[mine] * 2,
            out_shape=[flat, flat],
            input_output_aliases={4: 0, 5: 1},
            compiler_params=params("arbitrary"),
            cost_estimate=LARGE if last < coefs else SMALL,
            name="edge_terms",
        )(keep(late_res), keep(late_jac), keep(low_edge), keep(high_edge), residual, product)
    return residual.reshape(displacement.shape), product.reshape(displacement.shape)


def solution(mesh):
    placed = (
        P("harm", None, "mesh", None, None),
        P("harm", None, "mesh", None, None),
        P("harm", None, "mesh", None, None),
        P("mesh", None, None),
        P("mesh", None, None),
        P("mesh"),
        P("mesh"),
        P(None, "mesh"),
        P("harm", "mesh"),
        P("mesh"),
    )
    return jax.shard_map(
        on_device,
        mesh=mesh,
        in_specs=placed,
        out_specs=(P("harm", None, "mesh", None, None), P("harm", None, "mesh", None, None)),
        check_vma=False,
    )
```

```python
import math

import jax
import jax.numpy as jnp
import numpy as np
from jax import lax
from jax.experimental import pallas as pl
from jax.experimental.pallas import tpu as pltpu
from jax.sharding import PartitionSpec as P

HARM = 16
TIME = 64
LANES = 128

damping_ratio = 0.3
normal_penalty = 2.0
shear_penalty = 1.0

CUTS = ((3, 0), (3, 4), (7, 7), (8, 8))
VMEM = 28 * 1024 * 1024


def split2(value):
    high = value.astype(jnp.bfloat16)
    low = (value - high.astype(jnp.float32)).astype(jnp.bfloat16)
    return high, low


def split3(value):
    high = value.astype(jnp.bfloat16)
    rest = value - high.astype(jnp.float32)
    mid = rest.astype(jnp.bfloat16)
    low = (rest - mid.astype(jnp.float32)).astype(jnp.bfloat16)
    return high, mid, low


def slot_cells(cells_ref, send_ref):
    rows = cells_ref.shape[0]
    send = send_ref[...]
    high = send // LANES
    low = send % LANES
    found = jnp.zeros_like(send)
    for row in range(rows):
        table = jnp.broadcast_to(cells_ref[row : row + 1, :], send.shape)
        picked = jnp.take_along_axis(table, low, axis=1)
        found = jnp.where(high == row, picked, found)
    return jnp.concatenate([found[row : row + 1, :] for row in range(rows)], axis=1)


def one_hot_rows(index_row, count, kind):
    shape = (count, index_row.shape[1])
    hit = lax.broadcasted_iota(jnp.int32, shape, 0) == index_row
    return jnp.where(hit, 1.0, 0.0).astype(kind)


def gather_kernel(cells_ref, send_ref, x_ref, y_ref, out_ref, *refs, edges):
    edge_refs = refs[: len(edges)]
    cell_ref, low_ref = refs[len(edges) :]
    comp = pl.program_id(0)
    coefs, _, rows, axial = x_ref.shape
    slots = cell_ref.shape[1]

    @pl.when(comp == 0)
    def _():
        cell = slot_cells(cells_ref, send_ref)
        cell_ref[...] = cell
        hot = one_hot_rows(cell % axial, axial, jnp.bfloat16)
        low_ref[0:axial, :] = hot
        low_ref[axial : 2 * axial, :] = hot

    row_of = cell_ref[...] // axial
    mask = lax.broadcasted_iota(jnp.int32, (rows, slots), 0) == row_of
    for field, ref in enumerate((x_ref, y_ref)):
        for edge_ref, (start, first, last) in zip(edge_refs, edges):
            edge_ref[field, :, 0] = ref[first:last, 0, start : start + rows // 2]
        flat = ref[...].reshape(coefs * rows, axial)
        high, low = split2(flat)
        picked = jnp.dot(
            jnp.concatenate([high, low], axis=1),
            low_ref[...],
            preferred_element_type=jnp.float32,
        ).reshape(coefs, rows, slots)
        values = jnp.sum(jnp.where(mask[None], picked, 0.0), axis=1)
        block = field * 3 + comp
        if len(out_ref.shape) == 4:
            cap = out_ref.shape[3]
            for owner in range(out_ref.shape[0]):
                out_ref[owner, block] = values[:, owner * cap : (owner + 1) * cap]
        else:
            out_ref[block] = values


def pair_table(pairs_ref, slots):
    count = pairs_ref.shape[1]
    place = lax.broadcasted_iota(jnp.int32, (slots, count), 0)
    side_a = jnp.where(place == pairs_ref[0:1, :], 1.0, 0.0)
    side_b = jnp.where(place == pairs_ref[1:2, :], 1.0, 0.0)
    return (side_a - side_b).astype(jnp.bfloat16)


def by_slot(ref, block):
    if len(ref.shape) == 3:
        return ref[block]
    return jnp.concatenate([ref[owner, block] for owner in range(ref.shape[0])], axis=1)


def mark_kernel(piece_ref, out_ref):
    del piece_ref
    out_ref[...] = jnp.zeros_like(out_ref)


def opening_kernel(pairs_ref, status_ref, mark_ref, arrived_ref, out_ref):
    del mark_ref
    arrived = jnp.concatenate([by_slot(arrived_ref, block) for block in range(6)], axis=0)
    values, slots = arrived.shape
    table = pair_table(pairs_ref, slots)
    total = None
    for part in split3(arrived):
        term = jnp.dot(part, table, preferred_element_type=jnp.float32)
        total = term if total is None else total + term
    out_ref[0:values, :] = total
    out_ref[values:, :] = status_ref[...].astype(jnp.float32)


def force_kernel(place_ref, pairs_ref, gap_ref, table_ref, back_ref, all_ref, out_ref):
    harm_count, total_rows, pairs = all_ref.shape
    coefs = table_ref.shape[1] // harm_count
    values = 6 * coefs
    back = back_ref[place_ref[0]]
    closed = jnp.concatenate([all_ref[g, values:total_rows, :] for g in range(harm_count)], axis=0)
    coef_rows = []
    for block in range(6):
        spread = jnp.concatenate(
            [all_ref[g, block * coefs : (block + 1) * coefs, :] for g in range(harm_count)], axis=0
        )
        opening = jnp.dot(
            table_ref[...], spread, precision=lax.Precision.HIGHEST, preferred_element_type=jnp.float32
        )
        if block == 0:
            opening = opening + gap_ref[...]
        kappa = normal_penalty if block % 3 == 0 else shear_penalty
        force = closed * kappa * opening
        coef_rows.append(
            jnp.dot(back, force, precision=lax.Precision.HIGHEST, preferred_element_type=jnp.float32)
        )
    coef_force = jnp.concatenate(coef_rows, axis=0)
    direct = len(out_ref.shape) == 4
    slots = out_ref.shape[0] * out_ref.shape[3] if direct else out_ref.shape[2]
    table = pair_table(pairs_ref, slots)
    total = None
    for part in split3(coef_force):
        term = lax.dot_general(
            part, table, (((1,), (1,)), ((), ())), preferred_element_type=jnp.float32
        )
        total = term if total is None else total + term
    for block in range(6):
        part = total[block * coefs : (block + 1) * coefs]
        if direct:
            cap = out_ref.shape[3]
            for owner in range(out_ref.shape[0]):
                out_ref[owner, block] = part[:, owner * cap : (owner + 1) * cap]
        else:
            out_ref[block] = part


def combine_kernel(place_ref, cells_ref, send_ref, back_ref, *refs, edges, late):
    piece_refs = refs[: len(edges)]
    stiff_ref, mass_ref, x_ref, y_ref, forcing_ref = refs[len(edges) : len(edges) + 5]
    res_ref, jac_ref, late_res_ref, late_jac_ref, cell_ref, low_ref = refs[len(edges) + 5 :]
    comp = pl.program_id(0)
    coefs, _, rows, axial = x_ref.shape
    slots = cell_ref.shape[1]
    layer = rows // 2
    @pl.when(comp == 0)
    def _():
        cell = slot_cells(cells_ref, send_ref)
        cell_ref[...] = cell
        low_ref[...] = one_hot_rows(cell % axial, axial, jnp.bfloat16)

    row_of = cell_ref[...] // axial
    mask = lax.broadcasted_iota(jnp.int32, (rows, slots), 0) == row_of
    row = lax.broadcasted_iota(jnp.int32, (rows, axial), 0) % layer
    column = lax.broadcasted_iota(jnp.int32, (rows, axial), 1)
    mass = mass_ref[...]
    stiff = 6.0 + stiff_ref[...]
    for field, (ref, out_ref, late_ref) in enumerate(
        ((x_ref, res_ref, late_res_ref), (y_ref, jac_ref, late_jac_ref))
    ):
        force = by_slot(back_ref, field * 3 + comp)
        contact = None
        for part in split2(force):
            wide = part.astype(jnp.float32)
            spread = jnp.where(mask[None], wide[:, None, :], 0.0).astype(jnp.bfloat16)
            term = lax.dot_general(
                spread.reshape(coefs * rows, slots),
                low_ref[...],
                (((1,), (1,)), ((), ())),
                preferred_element_type=jnp.float32,
            )
            contact = term if contact is None else contact + term
        contact = contact.reshape(coefs, rows, axial)
        for coef in range(coefs):
            harmonic = place_ref[0] * (coefs // 2) + (coef // 2 + 1)
            frequency = harmonic.astype(jnp.float32) * (1.5 / HARM)
            value = ref[coef, 0]
            turned = ref[coef + 1, 0] if coef % 2 == 0 else -ref[coef - 1, 0]
            near = jnp.where(row == 0, 0.0, jnp.roll(value, 1, axis=0))
            near = near + jnp.where(row == layer - 1, 0.0, jnp.roll(value, -1, axis=0))
            near = near + jnp.where(column == 0, 0.0, pltpu.roll(value, 1, axis=1))
            near = near + jnp.where(column == axial - 1, 0.0, pltpu.roll(value, axial - 1, axis=1))
            near = near + jnp.concatenate([value[layer:], value[:layer]], axis=0)
            result = (stiff - (frequency * frequency) * mass) * value - near
            result = result + (frequency * damping_ratio) * mass * turned + contact[coef]
            if field == 0:
                result = result - forcing_ref[coef, 0]
            parts = [result[:layer], result[layer:]]
            for piece_ref, (start, first, last) in zip(piece_refs, edges):
                if first <= coef < last:
                    side = 0 if start > 0 else 1
                    parts[side] = parts[side] - piece_ref[field, coef - first, 0]
            for side in (0, 1):
                rows_of = pl.ds(side * layer, layer)
                if coef < late:
                    out_ref[coef, 0, rows_of] = parts[side]
                else:
                    late_ref[coef - late, comp, rows_of] = parts[side]


def edge_kernel(late_res, late_jac, below, above, res_in, jac_in, res_ref, jac_ref, *refs, late, starts):
    del res_in, jac_in
    stage, sems = refs
    first = min(starts)
    count = stage.shape[1]
    layer = stage.shape[3] // 2
    copies = []
    for field, (late_ref, out_ref) in enumerate(((late_res, res_ref), (late_jac, jac_ref))):
        value = late_ref[first - late : first - late + count]
        for piece, start, side in ((below, starts[0], 0), (above, starts[1], 1)):
            rows = slice(side * layer, (side + 1) * layer)
            skip = start - first
            if skip > 0:
                stage[field, :skip, :, rows] = value[:skip, :, rows]
            stage[field, skip:, :, rows] = value[skip:, :, rows] - piece[field]
        copy = pltpu.make_async_copy(
            stage.at[field], out_ref.at[first : first + count], sems.at[field]
        )
        copy.start()
        copies.append(copy)
    for copy in copies:
        copy.wait()


def transform_table(time_count, coef_count):
    sample = np.arange(time_count)[:, None]
    coef = np.arange(coef_count)[None, :]
    angles = ((coef // 2 + 1) * sample % time_count) * (2.0 * math.pi / time_count)
    return np.where(coef % 2 == 0, np.cos(angles), np.sin(angles)).astype(np.float32)


SMALL = pl.CostEstimate(flops=1000, transcendentals=0, bytes_accessed=1000)
LARGE = pl.CostEstimate(flops=10**12, transcendentals=10**9, bytes_accessed=10**10)


def params(*semantics):
    return pltpu.CompilerParams(vmem_limit_bytes=VMEM, dimension_semantics=semantics or None)


def on_device(
    displacement,
    direction,
    forcing,
    stiffness,
    lumped_mass,
    face_cells,
    send_rows,
    pair_rows,
    status,
    crack_gap,
):
    coefs, comps, layers, radial, axial = displacement.shape
    rows = layers * radial
    slots = face_cells.shape[0]
    pairs = pair_rows.shape[1]
    owners = lax.axis_size("mesh")
    cap = slots // owners
    direct = cap % LANES == 0
    harm_count = lax.axis_size("harm")
    harm_index = lax.axis_index("harm")
    coef_total = coefs * harm_count
    place = jnp.reshape(harm_index, (1,)).astype(jnp.int32)
    f32 = jnp.float32
    values = 2 * comps * coefs
    wire = (owners, 6, coefs, cap) if direct else (6, coefs, slots)

    forward = [(i, (i + 1) % owners) for i in range(owners)]
    backward = [(target, source) for source, target in forward]
    ahead = lambda piece: lax.ppermute(piece, "mesh", forward)
    behind = lambda piece: lax.ppermute(piece, "mesh", backward)
    keep = lambda value: pltpu.with_memory_space_constraint(value, pltpu.VMEM)
    stay = lambda value: pltpu.with_memory_space_constraint(value, pltpu.HBM)

    groups = []
    done = [0, 0]
    for ends in CUTS:
        group = []
        for side, end in enumerate(ends):
            last = end * coefs // 8
            if last > done[side]:
                group.append((radial * (1 - side), done[side], last))
                done[side] = last
        groups.append(group)
    shift = lambda edge, piece: ahead(piece) if edge[0] > 0 else behind(piece)
    pieces = [
        [
            shift(
                edge,
                jnp.stack(
                    [
                        field[edge[1] : edge[2], :, edge[0] // radial]
                        for field in (displacement, direction)
                    ]
                ),
            )
            for edge in groups[0]
        ]
    ]

    x = displacement.reshape(coefs, comps, rows, axial)
    y = direction.reshape(coefs, comps, rows, axial)
    cells = face_cells.reshape(slots // LANES, LANES)
    send = send_rows.reshape(slots // LANES, LANES)
    whole = lambda shape: pl.BlockSpec(shape, lambda *_: (0,) * len(shape))
    scalar = pl.BlockSpec(memory_space=pltpu.SMEM)
    near_memory = pl.BlockSpec(memory_space=pltpu.VMEM)
    per_comp = pl.BlockSpec((coefs, 1, rows, axial), lambda comp: (0, comp, 0, 0))

    edges = [edge for group in groups[1:] for edge in group]
    edge_shapes = [(2, last - first, comps, radial, axial) for _, first, last in edges]
    outgoing, *sent = pl.pallas_call(
        lambda *refs: gather_kernel(*refs, edges=edges),
        grid=(comps,),
        in_specs=[whole(cells.shape), whole(send.shape), per_comp, per_comp],
        out_specs=[whole(wire)]
        + [
            pl.BlockSpec(shape[:2] + (1,) + shape[3:], lambda comp: (0, 0, comp, 0, 0))
            for shape in edge_shapes
        ],
        out_shape=[pltpu.HBM(shape, f32) for shape in [wire] + edge_shapes],
        scratch_shapes=[
            pltpu.VMEM((1, slots), jnp.int32),
            pltpu.VMEM((2 * axial, slots), jnp.bfloat16),
        ],
        compiler_params=params("arbitrary"),
        cost_estimate=SMALL,
        name="face_gather",
    )(cells, send, stay(x), stay(y))

    def exchange(block):
        if not direct:
            block = block.reshape(values, owners, cap).transpose(1, 0, 2)
        block = lax.all_to_all(block, "mesh", split_axis=0, concat_axis=0, tiled=True)
        if not direct:
            block = block.transpose(1, 0, 2).reshape(wire)
        return block

    queue = []
    for group in groups[1:]:
        queue.append(sent[: len(group)])
        sent = sent[len(group) :]
    send_group = lambda index: [
        shift(edge, piece) for edge, piece in zip(groups[index], queue[index - 1])
    ]
    outgoing, queue[0] = lax.optimization_barrier((outgoing, queue[0]))
    mark = pl.pallas_call(
        mark_kernel,
        in_specs=[pl.BlockSpec(memory_space=pl.ANY)],
        out_specs=near_memory,
        out_shape=pltpu.VMEM((8, LANES), f32),
        cost_estimate=LARGE,
        name="first_piece_arrived",
    )(pieces[0][-1])
    pieces.append(send_group(1))
    arrived = exchange(outgoing)
    own_opening = pl.pallas_call(
        opening_kernel,
        in_specs=[whole(pair_rows.shape), whole(status.shape), near_memory, near_memory],
        out_specs=whole((values + status.shape[0], pairs)),
        out_shape=jax.ShapeDtypeStruct((values + status.shape[0], pairs), f32),
        compiler_params=params(),
        cost_estimate=SMALL,
        name="pair_difference",
    )(pair_rows, status, keep(mark), pltpu.with_memory_space_constraint(arrived, pltpu.VMEM))
    everything = lax.all_gather(own_opening, "harm")
    table = transform_table(TIME, coef_total)
    back = ((2.0 / TIME) * table.T).reshape(harm_count, coefs, TIME)
    slot_force = pl.pallas_call(
        force_kernel,
        in_specs=[
            scalar,
            whole(pair_rows.shape),
            whole((1, pairs)),
            whole(table.shape),
            whole(back.shape),
            whole(everything.shape),
        ],
        out_specs=whole(wire),
        out_shape=jax.ShapeDtypeStruct(wire, f32),
        compiler_params=params(),
        cost_estimate=LARGE,
        name="pair_force",
    )(place, pair_rows, crack_gap.reshape(1, pairs), jnp.asarray(table), jnp.asarray(back), everything)
    returned = exchange(slot_force)
    pieces[1], queue[1:], _ = lax.optimization_barrier((pieces[1], queue[1:], slot_force))
    pieces.append(send_group(2))

    flat = jax.ShapeDtypeStruct(x.shape, f32)
    piece_spec = lambda piece: pl.BlockSpec(
        piece.shape[:2] + (1,) + piece.shape[3:], lambda comp: (0, 0, comp, 0, 0)
    )
    early = groups[0] + groups[1]
    late = min(group[1] for group in groups[2])
    late_shape = pltpu.VMEM((coefs - late, comps, rows, axial), f32)
    residual, product, late_res, late_jac = pl.pallas_call(
        lambda *refs: combine_kernel(*refs, edges=early, late=late),
        grid=(comps,),
        in_specs=[scalar, whole(cells.shape), whole(send.shape)]
        + [near_memory]
        + [piece_spec(piece) for piece in pieces[0] + pieces[1]]
        + [whole((rows, axial))] * 2
        + [per_comp] * 3,
        out_specs=[per_comp] * 2 + [near_memory] * 2,
        out_shape=[flat, flat, late_shape, late_shape],
        scratch_shapes=[
            pltpu.VMEM((1, slots), jnp.int32),
            pltpu.VMEM((axial, slots), jnp.bfloat16),
        ],
        compiler_params=params("arbitrary"),
        cost_estimate=LARGE,
        name="combine_terms",
    )(
        place,
        cells,
        send,
        keep(returned),
        *pieces[0],
        *pieces[1],
        stiffness.reshape(rows, axial),
        lumped_mass.reshape(rows, axial),
        stay(x),
        stay(y),
        stay(forcing.reshape(x.shape)),
    )
    residual, queue[2] = lax.optimization_barrier((residual, queue[2]))
    pieces.append(send_group(3))

    for group, piece in zip(groups[2:], pieces[2:]):
        starts = [edge[1] for edge in group]
        last = group[0][2]
        residual, product = pl.pallas_call(
            lambda *refs, starts=starts: edge_kernel(*refs, late=late, starts=starts),
            in_specs=[near_memory] * 4 + [pl.BlockSpec(memory_space=pl.ANY)] * 2,
            out_specs=[pl.BlockSpec(memory_space=pl.ANY)] * 2,
            out_shape=[flat, flat],
            input_output_aliases={4: 0, 5: 1},
            scratch_shapes=[
                pltpu.VMEM((2, last - min(starts), comps, rows, axial), f32),
                pltpu.SemaphoreType.DMA((2,)),
            ],
            compiler_params=params(),
            cost_estimate=LARGE if last < coefs else SMALL,
            name="edge_terms",
        )(keep(late_res), keep(late_jac), *[keep(value) for value in piece], residual, product)
    return residual.reshape(displacement.shape), product.reshape(displacement.shape)


def solution(mesh):
    placed = (
        P("harm", None, "mesh", None, None),
        P("harm", None, "mesh", None, None),
        P("harm", None, "mesh", None, None),
        P("mesh", None, None),
        P("mesh", None, None),
        P("mesh"),
        P("mesh"),
        P(None, "mesh"),
        P("harm", "mesh"),
        P("mesh"),
    )
    return jax.shard_map(
        on_device,
        mesh=mesh,
        in_specs=placed,
        out_specs=(P("harm", None, "mesh", None, None), P("harm", None, "mesh", None, None)),
        check_vma=False,
    )
```

```python
import math

import jax
import jax.numpy as jnp
import numpy as np
from jax import lax
from jax.experimental import pallas as pl
from jax.experimental.pallas import tpu as pltpu
from jax.sharding import PartitionSpec as P

HARM = 16
TIME = 64
LANES = 128

damping_ratio = 0.3
normal_penalty = 2.0
shear_penalty = 1.0

CUTS = ((3, 0), (3, 5), (7, 7), (8, 8))
VMEM = 28 * 1024 * 1024


def split2(value):
    high = value.astype(jnp.bfloat16)
    low = (value - high.astype(jnp.float32)).astype(jnp.bfloat16)
    return high, low


def split3(value):
    high = value.astype(jnp.bfloat16)
    rest = value - high.astype(jnp.float32)
    mid = rest.astype(jnp.bfloat16)
    low = (rest - mid.astype(jnp.float32)).astype(jnp.bfloat16)
    return high, mid, low


def slot_cells(cells_ref, send_ref):
    rows = cells_ref.shape[0]
    send = send_ref[...]
    high = send // LANES
    low = send % LANES
    found = jnp.zeros_like(send)
    for row in range(rows):
        table = jnp.broadcast_to(cells_ref[row : row + 1, :], send.shape)
        picked = jnp.take_along_axis(table, low, axis=1)
        found = jnp.where(high == row, picked, found)
    return jnp.concatenate([found[row : row + 1, :] for row in range(rows)], axis=1)


def one_hot_rows(index_row, count, kind):
    shape = (count, index_row.shape[1])
    hit = lax.broadcasted_iota(jnp.int32, shape, 0) == index_row
    return jnp.where(hit, 1.0, 0.0).astype(kind)


def gather_kernel(cells_ref, send_ref, x_ref, y_ref, out_ref, *refs, edges):
    edge_refs = refs[: len(edges)]
    cell_ref, low_ref = refs[len(edges) :]
    comp = pl.program_id(0)
    coefs, _, rows, axial = x_ref.shape
    slots = cell_ref.shape[1]

    @pl.when(comp == 0)
    def _():
        cell = slot_cells(cells_ref, send_ref)
        cell_ref[...] = cell
        hot = one_hot_rows(cell % axial, axial, jnp.bfloat16)
        low_ref[0:axial, :] = hot
        low_ref[axial : 2 * axial, :] = hot

    row_of = cell_ref[...] // axial
    mask = lax.broadcasted_iota(jnp.int32, (rows, slots), 0) == row_of
    for field, ref in enumerate((x_ref, y_ref)):
        for edge_ref, (start, first, last) in zip(edge_refs, edges):
            edge_ref[field, :, 0] = ref[first:last, 0, start : start + rows // 2]
        flat = ref[...].reshape(coefs * rows, axial)
        high, low = split2(flat)
        picked = jnp.dot(
            jnp.concatenate([high, low], axis=1),
            low_ref[...],
            preferred_element_type=jnp.float32,
        ).reshape(coefs, rows, slots)
        values = jnp.sum(jnp.where(mask[None], picked, 0.0), axis=1)
        block = field * 3 + comp
        if len(out_ref.shape) == 4:
            cap = out_ref.shape[3]
            for owner in range(out_ref.shape[0]):
                out_ref[owner, block] = values[:, owner * cap : (owner + 1) * cap]
        else:
            out_ref[block] = values


def pair_table(pairs_ref, slots):
    count = pairs_ref.shape[1]
    place = lax.broadcasted_iota(jnp.int32, (slots, count), 0)
    side_a = jnp.where(place == pairs_ref[0:1, :], 1.0, 0.0)
    side_b = jnp.where(place == pairs_ref[1:2, :], 1.0, 0.0)
    return (side_a - side_b).astype(jnp.bfloat16)


def by_slot(ref, block):
    if len(ref.shape) == 3:
        return ref[block]
    return jnp.concatenate([ref[owner, block] for owner in range(ref.shape[0])], axis=1)


def mark_kernel(piece_ref, out_ref):
    del piece_ref
    out_ref[...] = jnp.zeros_like(out_ref)


def opening_kernel(pairs_ref, status_ref, mark_ref, arrived_ref, out_ref):
    del mark_ref
    arrived = jnp.concatenate([by_slot(arrived_ref, block) for block in range(6)], axis=0)
    values, slots = arrived.shape
    table = pair_table(pairs_ref, slots)
    total = None
    for part in split3(arrived):
        term = jnp.dot(part, table, preferred_element_type=jnp.float32)
        total = term if total is None else total + term
    out_ref[0:values, :] = total
    out_ref[values:, :] = status_ref[...].astype(jnp.float32)


def force_kernel(place_ref, pairs_ref, gap_ref, table_ref, back_ref, all_ref, out_ref):
    harm_count, total_rows, pairs = all_ref.shape
    coefs = table_ref.shape[1] // harm_count
    values = 6 * coefs
    back = back_ref[place_ref[0]]
    closed = jnp.concatenate([all_ref[g, values:total_rows, :] for g in range(harm_count)], axis=0)
    coef_rows = []
    for block in range(6):
        spread = jnp.concatenate(
            [all_ref[g, block * coefs : (block + 1) * coefs, :] for g in range(harm_count)], axis=0
        )
        opening = jnp.dot(
            table_ref[...], spread, precision=lax.Precision.HIGHEST, preferred_element_type=jnp.float32
        )
        if block == 0:
            opening = opening + gap_ref[...]
        kappa = normal_penalty if block % 3 == 0 else shear_penalty
        force = closed * kappa * opening
        coef_rows.append(
            jnp.dot(back, force, precision=lax.Precision.HIGHEST, preferred_element_type=jnp.float32)
        )
    coef_force = jnp.concatenate(coef_rows, axis=0)
    direct = len(out_ref.shape) == 4
    slots = out_ref.shape[0] * out_ref.shape[3] if direct else out_ref.shape[2]
    table = pair_table(pairs_ref, slots)
    total = None
    for part in split3(coef_force):
        term = lax.dot_general(
            part, table, (((1,), (1,)), ((), ())), preferred_element_type=jnp.float32
        )
        total = term if total is None else total + term
    for block in range(6):
        part = total[block * coefs : (block + 1) * coefs]
        if direct:
            cap = out_ref.shape[3]
            for owner in range(out_ref.shape[0]):
                out_ref[owner, block] = part[:, owner * cap : (owner + 1) * cap]
        else:
            out_ref[block] = part


def combine_kernel(mark_ref, place_ref, cells_ref, send_ref, back_ref, *refs, edges, late):
    del mark_ref
    piece_refs = refs[: len(edges)]
    stiff_ref, mass_ref, x_ref, y_ref, forcing_ref = refs[len(edges) : len(edges) + 5]
    res_ref, jac_ref, late_res_ref, late_jac_ref, cell_ref, low_ref = refs[len(edges) + 5 :]
    comp = pl.program_id(0)
    coefs, _, rows, axial = x_ref.shape
    slots = cell_ref.shape[1]
    layer = rows // 2
    @pl.when(comp == 0)
    def _():
        cell = slot_cells(cells_ref, send_ref)
        cell_ref[...] = cell
        low_ref[...] = one_hot_rows(cell % axial, axial, jnp.bfloat16)

    row_of = cell_ref[...] // axial
    mask = lax.broadcasted_iota(jnp.int32, (rows, slots), 0) == row_of
    row = lax.broadcasted_iota(jnp.int32, (rows, axial), 0) % layer
    column = lax.broadcasted_iota(jnp.int32, (rows, axial), 1)
    mass = mass_ref[...]
    stiff = 6.0 + stiff_ref[...]
    for field, (ref, out_ref, late_ref) in enumerate(
        ((x_ref, res_ref, late_res_ref), (y_ref, jac_ref, late_jac_ref))
    ):
        force = by_slot(back_ref, field * 3 + comp)
        contact = None
        for part in split2(force):
            wide = part.astype(jnp.float32)
            spread = jnp.where(mask[None], wide[:, None, :], 0.0).astype(jnp.bfloat16)
            term = lax.dot_general(
                spread.reshape(coefs * rows, slots),
                low_ref[...],
                (((1,), (1,)), ((), ())),
                preferred_element_type=jnp.float32,
            )
            contact = term if contact is None else contact + term
        contact = contact.reshape(coefs, rows, axial)
        for coef in range(coefs):
            harmonic = place_ref[0] * (coefs // 2) + (coef // 2 + 1)
            frequency = harmonic.astype(jnp.float32) * (1.5 / HARM)
            value = ref[coef, 0]
            turned = ref[coef + 1, 0] if coef % 2 == 0 else -ref[coef - 1, 0]
            near = jnp.where(row == 0, 0.0, jnp.roll(value, 1, axis=0))
            near = near + jnp.where(row == layer - 1, 0.0, jnp.roll(value, -1, axis=0))
            near = near + jnp.where(column == 0, 0.0, pltpu.roll(value, 1, axis=1))
            near = near + jnp.where(column == axial - 1, 0.0, pltpu.roll(value, axial - 1, axis=1))
            near = near + jnp.concatenate([value[layer:], value[:layer]], axis=0)
            result = (stiff - (frequency * frequency) * mass) * value - near
            result = result + (frequency * damping_ratio) * mass * turned + contact[coef]
            if field == 0:
                result = result - forcing_ref[coef, 0]
            parts = [result[:layer], result[layer:]]
            for piece_ref, (start, first, last) in zip(piece_refs, edges):
                if first <= coef < last:
                    side = 0 if start > 0 else 1
                    parts[side] = parts[side] - piece_ref[field, coef - first, 0]
            for side in (0, 1):
                rows_of = pl.ds(side * layer, layer)
                if coef < late:
                    out_ref[coef, 0, rows_of] = parts[side]
                else:
                    late_ref[coef - late, comp, rows_of] = parts[side]


def edge_kernel(late_res, late_jac, below, above, res_in, jac_in, res_ref, jac_ref, *refs, late, starts):
    del res_in, jac_in
    stage, sems = refs
    first = min(starts)
    count = stage.shape[1]
    layer = stage.shape[3] // 2
    copies = []
    for field, (late_ref, out_ref) in enumerate(((late_res, res_ref), (late_jac, jac_ref))):
        value = late_ref[first - late : first - late + count]
        for piece, start, side in ((below, starts[0], 0), (above, starts[1], 1)):
            rows = slice(side * layer, (side + 1) * layer)
            skip = start - first
            if skip > 0:
                stage[field, :skip, :, rows] = value[:skip, :, rows]
            stage[field, skip:, :, rows] = value[skip:, :, rows] - piece[field]
        copy = pltpu.make_async_copy(
            stage.at[field], out_ref.at[first : first + count], sems.at[field]
        )
        copy.start()
        copies.append(copy)
    for copy in copies:
        copy.wait()


def transform_table(time_count, coef_count):
    sample = np.arange(time_count)[:, None]
    coef = np.arange(coef_count)[None, :]
    angles = ((coef // 2 + 1) * sample % time_count) * (2.0 * math.pi / time_count)
    return np.where(coef % 2 == 0, np.cos(angles), np.sin(angles)).astype(np.float32)


SMALL = pl.CostEstimate(flops=1000, transcendentals=0, bytes_accessed=1000)
LARGE = pl.CostEstimate(flops=10**12, transcendentals=10**9, bytes_accessed=10**10)


def params(*semantics):
    return pltpu.CompilerParams(vmem_limit_bytes=VMEM, dimension_semantics=semantics or None)


def on_device(
    displacement,
    direction,
    forcing,
    stiffness,
    lumped_mass,
    face_cells,
    send_rows,
    pair_rows,
    status,
    crack_gap,
):
    coefs, comps, layers, radial, axial = displacement.shape
    rows = layers * radial
    slots = face_cells.shape[0]
    pairs = pair_rows.shape[1]
    owners = lax.axis_size("mesh")
    cap = slots // owners
    direct = cap % LANES == 0
    harm_count = lax.axis_size("harm")
    harm_index = lax.axis_index("harm")
    coef_total = coefs * harm_count
    place = jnp.reshape(harm_index, (1,)).astype(jnp.int32)
    f32 = jnp.float32
    values = 2 * comps * coefs
    wire = (owners, 6, coefs, cap) if direct else (6, coefs, slots)

    forward = [(i, (i + 1) % owners) for i in range(owners)]
    backward = [(target, source) for source, target in forward]
    ahead = lambda piece: lax.ppermute(piece, "mesh", forward)
    behind = lambda piece: lax.ppermute(piece, "mesh", backward)
    keep = lambda value: pltpu.with_memory_space_constraint(value, pltpu.VMEM)
    stay = lambda value: pltpu.with_memory_space_constraint(value, pltpu.HBM)

    groups = []
    done = [0, 0]
    for ends in CUTS:
        group = []
        for side, end in enumerate(ends):
            last = end * coefs // 8
            if last > done[side]:
                group.append((radial * (1 - side), done[side], last))
                done[side] = last
        groups.append(group)
    shift = lambda edge, piece: ahead(piece) if edge[0] > 0 else behind(piece)
    pieces = [
        [
            shift(
                edge,
                jnp.stack(
                    [
                        field[edge[1] : edge[2], :, edge[0] // radial]
                        for field in (displacement, direction)
                    ]
                ),
            )
            for edge in groups[0]
        ]
    ]

    x = displacement.reshape(coefs, comps, rows, axial)
    y = direction.reshape(coefs, comps, rows, axial)
    cells = face_cells.reshape(slots // LANES, LANES)
    send = send_rows.reshape(slots // LANES, LANES)
    whole = lambda shape: pl.BlockSpec(shape, lambda *_: (0,) * len(shape))
    scalar = pl.BlockSpec(memory_space=pltpu.SMEM)
    near_memory = pl.BlockSpec(memory_space=pltpu.VMEM)
    per_comp = pl.BlockSpec((coefs, 1, rows, axial), lambda comp: (0, comp, 0, 0))

    edges = [edge for group in groups[1:] for edge in group]
    edge_shapes = [(2, last - first, comps, radial, axial) for _, first, last in edges]
    outgoing, *sent = pl.pallas_call(
        lambda *refs: gather_kernel(*refs, edges=edges),
        grid=(comps,),
        in_specs=[whole(cells.shape), whole(send.shape), per_comp, per_comp],
        out_specs=[whole(wire)]
        + [
            pl.BlockSpec(shape[:2] + (1,) + shape[3:], lambda comp: (0, 0, comp, 0, 0))
            for shape in edge_shapes
        ],
        out_shape=[pltpu.HBM(shape, f32) for shape in [wire] + edge_shapes],
        scratch_shapes=[
            pltpu.VMEM((1, slots), jnp.int32),
            pltpu.VMEM((2 * axial, slots), jnp.bfloat16),
        ],
        compiler_params=params("arbitrary"),
        cost_estimate=SMALL,
        name="face_gather",
    )(cells, send, stay(x), stay(y))

    def exchange(block):
        if not direct:
            block = block.reshape(values, owners, cap).transpose(1, 0, 2)
        block = lax.all_to_all(block, "mesh", split_axis=0, concat_axis=0, tiled=True)
        if not direct:
            block = block.transpose(1, 0, 2).reshape(wire)
        return block

    queue = []
    for group in groups[1:]:
        queue.append(sent[: len(group)])
        sent = sent[len(group) :]
    send_group = lambda index: [
        shift(edge, piece) for edge, piece in zip(groups[index], queue[index - 1])
    ]
    outgoing, queue[0] = lax.optimization_barrier((outgoing, queue[0]))
    arrival = pl.pallas_call(
        mark_kernel,
        in_specs=[pl.BlockSpec(memory_space=pl.ANY)],
        out_specs=near_memory,
        out_shape=pltpu.VMEM((8, LANES), f32),
        cost_estimate=LARGE,
        name="piece_arrived",
    )
    mark = arrival(pieces[0][-1])
    pieces.append(send_group(1))
    arrived = exchange(outgoing)
    own_opening = pl.pallas_call(
        opening_kernel,
        in_specs=[whole(pair_rows.shape), whole(status.shape), near_memory, near_memory],
        out_specs=whole((values + status.shape[0], pairs)),
        out_shape=jax.ShapeDtypeStruct((values + status.shape[0], pairs), f32),
        compiler_params=params(),
        cost_estimate=SMALL,
        name="pair_difference",
    )(pair_rows, status, keep(mark), pltpu.with_memory_space_constraint(arrived, pltpu.VMEM))
    everything = lax.all_gather(own_opening, "harm")
    table = transform_table(TIME, coef_total)
    back = ((2.0 / TIME) * table.T).reshape(harm_count, coefs, TIME)
    slot_force = pl.pallas_call(
        force_kernel,
        in_specs=[
            scalar,
            whole(pair_rows.shape),
            whole((1, pairs)),
            whole(table.shape),
            whole(back.shape),
            whole(everything.shape),
        ],
        out_specs=whole(wire),
        out_shape=jax.ShapeDtypeStruct(wire, f32),
        compiler_params=params(),
        cost_estimate=LARGE,
        name="pair_force",
    )(place, pair_rows, crack_gap.reshape(1, pairs), jnp.asarray(table), jnp.asarray(back), everything)
    returned = exchange(slot_force)
    queue[1:], _ = lax.optimization_barrier((queue[1:], slot_force))
    second_mark = arrival(pieces[1][-1])
    pieces.append(send_group(2))

    flat = jax.ShapeDtypeStruct(x.shape, f32)
    piece_spec = lambda piece: pl.BlockSpec(
        piece.shape[:2] + (1,) + piece.shape[3:], lambda comp: (0, 0, comp, 0, 0)
    )
    early = groups[0] + groups[1]
    late = min(group[1] for group in groups[2])
    late_shape = pltpu.VMEM((coefs - late, comps, rows, axial), f32)
    residual, product, late_res, late_jac = pl.pallas_call(
        lambda *refs: combine_kernel(*refs, edges=early, late=late),
        grid=(comps,),
        in_specs=[near_memory, scalar, whole(cells.shape), whole(send.shape)]
        + [near_memory]
        + [piece_spec(piece) for piece in pieces[0] + pieces[1]]
        + [whole((rows, axial))] * 2
        + [per_comp] * 3,
        out_specs=[per_comp] * 2 + [near_memory] * 2,
        out_shape=[flat, flat, late_shape, late_shape],
        scratch_shapes=[
            pltpu.VMEM((1, slots), jnp.int32),
            pltpu.VMEM((axial, slots), jnp.bfloat16),
        ],
        compiler_params=params("arbitrary"),
        cost_estimate=SMALL,
        name="combine_terms",
    )(
        keep(second_mark),
        place,
        cells,
        send,
        keep(returned),
        *pieces[0],
        *pieces[1],
        stiffness.reshape(rows, axial),
        lumped_mass.reshape(rows, axial),
        stay(x),
        stay(y),
        stay(forcing.reshape(x.shape)),
    )
    residual, queue[2] = lax.optimization_barrier((residual, queue[2]))
    pieces.append(send_group(3))

    for group, piece in zip(groups[2:], pieces[2:]):
        starts = [edge[1] for edge in group]
        last = group[0][2]
        residual, product = pl.pallas_call(
            lambda *refs, starts=starts: edge_kernel(*refs, late=late, starts=starts),
            in_specs=[near_memory] * 4 + [pl.BlockSpec(memory_space=pl.ANY)] * 2,
            out_specs=[pl.BlockSpec(memory_space=pl.ANY)] * 2,
            out_shape=[flat, flat],
            input_output_aliases={4: 0, 5: 1},
            scratch_shapes=[
                pltpu.VMEM((2, last - min(starts), comps, rows, axial), f32),
                pltpu.SemaphoreType.DMA((2,)),
            ],
            compiler_params=params(),
            cost_estimate=LARGE if last < coefs else SMALL,
            name="edge_terms",
        )(keep(late_res), keep(late_jac), *[keep(value) for value in piece], residual, product)
    return residual.reshape(displacement.shape), product.reshape(displacement.shape)


def solution(mesh):
    placed = (
        P("harm", None, "mesh", None, None),
        P("harm", None, "mesh", None, None),
        P("harm", None, "mesh", None, None),
        P("mesh", None, None),
        P("mesh", None, None),
        P("mesh"),
        P("mesh"),
        P(None, "mesh"),
        P("harm", "mesh"),
        P("mesh"),
    )
    return jax.shard_map(
        on_device,
        mesh=mesh,
        in_specs=placed,
        out_specs=(P("harm", None, "mesh", None, None), P("harm", None, "mesh", None, None)),
        check_vma=False,
    )
```

```python
import math

import jax
import jax.numpy as jnp
import numpy as np
from jax import lax
from jax.experimental import pallas as pl
from jax.experimental.pallas import tpu as pltpu
from jax.sharding import PartitionSpec as P

HARM = 16
TIME = 64
LANES = 128

damping_ratio = 0.3
normal_penalty = 2.0
shear_penalty = 1.0

CUTS = ((3, 0), (3, 5), (7, 7), (8, 8))
VMEM = 28 * 1024 * 1024


def split2(value):
    high = value.astype(jnp.bfloat16)
    low = (value - high.astype(jnp.float32)).astype(jnp.bfloat16)
    return high, low


def split3(value):
    high = value.astype(jnp.bfloat16)
    rest = value - high.astype(jnp.float32)
    mid = rest.astype(jnp.bfloat16)
    low = (rest - mid.astype(jnp.float32)).astype(jnp.bfloat16)
    return high, mid, low


def slot_cells(cells_ref, send_ref):
    rows = cells_ref.shape[0]
    send = send_ref[...]
    high = send // LANES
    low = send % LANES
    found = jnp.zeros_like(send)
    for row in range(rows):
        table = jnp.broadcast_to(cells_ref[row : row + 1, :], send.shape)
        picked = jnp.take_along_axis(table, low, axis=1)
        found = jnp.where(high == row, picked, found)
    return jnp.concatenate([found[row : row + 1, :] for row in range(rows)], axis=1)


def one_hot_rows(index_row, count, kind):
    shape = (count, index_row.shape[1])
    hit = lax.broadcasted_iota(jnp.int32, shape, 0) == index_row
    return jnp.where(hit, 1.0, 0.0).astype(kind)


def gather_kernel(cells_ref, send_ref, x_ref, y_ref, out_ref, *refs, edges):
    edge_refs = refs[: len(edges)]
    cell_ref, low_ref = refs[len(edges) :]
    comp = pl.program_id(0)
    coefs, _, rows, axial = x_ref.shape
    slots = cell_ref.shape[1]

    @pl.when(comp == 0)
    def _():
        cell = slot_cells(cells_ref, send_ref)
        cell_ref[...] = cell
        hot = one_hot_rows(cell % axial, axial, jnp.bfloat16)
        low_ref[0:axial, :] = hot
        low_ref[axial : 2 * axial, :] = hot

    row_of = cell_ref[...] // axial
    mask = lax.broadcasted_iota(jnp.int32, (rows, slots), 0) == row_of
    for field, ref in enumerate((x_ref, y_ref)):
        for edge_ref, (start, first, last) in zip(edge_refs, edges):
            edge_ref[field, :, 0] = ref[first:last, 0, start : start + rows // 2]
        flat = ref[...].reshape(coefs * rows, axial)
        high, low = split2(flat)
        picked = jnp.dot(
            jnp.concatenate([high, low], axis=1),
            low_ref[...],
            preferred_element_type=jnp.float32,
        ).reshape(coefs, rows, slots)
        values = jnp.sum(jnp.where(mask[None], picked, 0.0), axis=1)
        block = field * 3 + comp
        if len(out_ref.shape) == 4:
            cap = out_ref.shape[3]
            for owner in range(out_ref.shape[0]):
                out_ref[owner, block] = values[:, owner * cap : (owner + 1) * cap]
        else:
            out_ref[block] = values


def pair_table(pairs_ref, slots):
    count = pairs_ref.shape[1]
    place = lax.broadcasted_iota(jnp.int32, (slots, count), 0)
    side_a = jnp.where(place == pairs_ref[0:1, :], 1.0, 0.0)
    side_b = jnp.where(place == pairs_ref[1:2, :], 1.0, 0.0)
    return (side_a - side_b).astype(jnp.bfloat16)


def by_slot(ref, block):
    if len(ref.shape) == 3:
        return ref[block]
    return jnp.concatenate([ref[owner, block] for owner in range(ref.shape[0])], axis=1)


def mark_kernel(piece_ref, out_ref):
    del piece_ref
    out_ref[...] = jnp.zeros_like(out_ref)


def opening_kernel(pairs_ref, status_ref, mark_ref, arrived_ref, out_ref):
    del mark_ref
    arrived = jnp.concatenate([by_slot(arrived_ref, block) for block in range(6)], axis=0)
    values, slots = arrived.shape
    table = pair_table(pairs_ref, slots)
    total = None
    for part in split3(arrived):
        term = jnp.dot(part, table, preferred_element_type=jnp.float32)
        total = term if total is None else total + term
    out_ref[0:values, :] = total
    out_ref[values:, :] = status_ref[...].astype(jnp.float32)


def force_kernel(place_ref, pairs_ref, gap_ref, table_ref, back_ref, all_ref, out_ref):
    harm_count, total_rows, pairs = all_ref.shape
    coefs = table_ref.shape[1] // harm_count
    values = 6 * coefs
    back = back_ref[place_ref[0]]
    closed = jnp.concatenate([all_ref[g, values:total_rows, :] for g in range(harm_count)], axis=0)
    coef_rows = []
    for block in range(6):
        spread = jnp.concatenate(
            [all_ref[g, block * coefs : (block + 1) * coefs, :] for g in range(harm_count)], axis=0
        )
        opening = jnp.dot(
            table_ref[...], spread, precision=lax.Precision.HIGHEST, preferred_element_type=jnp.float32
        )
        if block == 0:
            opening = opening + gap_ref[...]
        kappa = normal_penalty if block % 3 == 0 else shear_penalty
        force = closed * kappa * opening
        coef_rows.append(
            jnp.dot(back, force, precision=lax.Precision.HIGHEST, preferred_element_type=jnp.float32)
        )
    coef_force = jnp.concatenate(coef_rows, axis=0)
    direct = len(out_ref.shape) == 4
    slots = out_ref.shape[0] * out_ref.shape[3] if direct else out_ref.shape[2]
    table = pair_table(pairs_ref, slots)
    total = None
    for part in split3(coef_force):
        term = lax.dot_general(
            part, table, (((1,), (1,)), ((), ())), preferred_element_type=jnp.float32
        )
        total = term if total is None else total + term
    for block in range(6):
        part = total[block * coefs : (block + 1) * coefs]
        if direct:
            cap = out_ref.shape[3]
            for owner in range(out_ref.shape[0]):
                out_ref[owner, block] = part[:, owner * cap : (owner + 1) * cap]
        else:
            out_ref[block] = part


def combine_kernel(mark_ref, place_ref, cells_ref, send_ref, back_ref, *refs, edges, late):
    del mark_ref
    piece_refs = refs[: len(edges)]
    stiff_ref, mass_ref, x_ref, y_ref, forcing_ref = refs[len(edges) : len(edges) + 5]
    res_ref, jac_ref, late_res_ref, late_jac_ref, cell_ref, low_ref = refs[len(edges) + 5 :]
    comp = pl.program_id(0)
    coefs, _, rows, axial = x_ref.shape
    slots = cell_ref.shape[1]
    layer = rows // 2
    @pl.when(comp == 0)
    def _():
        cell = slot_cells(cells_ref, send_ref)
        cell_ref[...] = cell
        low_ref[...] = one_hot_rows(cell % axial, axial, jnp.bfloat16)

    row_of = cell_ref[...] // axial
    mask = lax.broadcasted_iota(jnp.int32, (rows, slots), 0) == row_of
    row = lax.broadcasted_iota(jnp.int32, (rows, axial), 0) % layer
    column = lax.broadcasted_iota(jnp.int32, (rows, axial), 1)
    mass = mass_ref[...]
    stiff = 6.0 + stiff_ref[...]
    for field, (ref, out_ref, late_ref) in enumerate(
        ((x_ref, res_ref, late_res_ref), (y_ref, jac_ref, late_jac_ref))
    ):
        force = by_slot(back_ref, field * 3 + comp)
        contact = None
        for part in split2(force):
            wide = part.astype(jnp.float32)
            spread = jnp.where(mask[None], wide[:, None, :], 0.0).astype(jnp.bfloat16)
            term = lax.dot_general(
                spread.reshape(coefs * rows, slots),
                low_ref[...],
                (((1,), (1,)), ((), ())),
                preferred_element_type=jnp.float32,
            )
            contact = term if contact is None else contact + term
        contact = contact.reshape(coefs, rows, axial)
        for coef in range(coefs):
            harmonic = place_ref[0] * (coefs // 2) + (coef // 2 + 1)
            frequency = harmonic.astype(jnp.float32) * (1.5 / HARM)
            value = ref[coef, 0]
            turned = ref[coef + 1, 0] if coef % 2 == 0 else -ref[coef - 1, 0]
            near = jnp.where(row == 0, 0.0, jnp.roll(value, 1, axis=0))
            near = near + jnp.where(row == layer - 1, 0.0, jnp.roll(value, -1, axis=0))
            near = near + jnp.where(column == 0, 0.0, pltpu.roll(value, 1, axis=1))
            near = near + jnp.where(column == axial - 1, 0.0, pltpu.roll(value, axial - 1, axis=1))
            near = near + jnp.concatenate([value[layer:], value[:layer]], axis=0)
            result = (stiff - (frequency * frequency) * mass) * value - near
            result = result + (frequency * damping_ratio) * mass * turned + contact[coef]
            if field == 0:
                result = result - forcing_ref[coef, 0]
            parts = [result[:layer], result[layer:]]
            for piece_ref, (start, first, last) in zip(piece_refs, edges):
                if first <= coef < last:
                    side = 0 if start > 0 else 1
                    parts[side] = parts[side] - piece_ref[field, coef - first, 0]
            for side in (0, 1):
                rows_of = pl.ds(side * layer, layer)
                if coef < late:
                    out_ref[coef, 0, rows_of] = parts[side]
                else:
                    late_ref[coef - late, comp, rows_of] = parts[side]


def edge_kernel(late_res, late_jac, below, above, res_in, jac_in, res_ref, jac_ref, *refs, late, starts):
    del res_in, jac_in
    stage, sems = refs
    first = min(starts)
    count = stage.shape[1]
    layer = stage.shape[3] // 2
    copies = []
    for coef in range(first, first + count):
        for field, (late_ref, out_ref) in enumerate(((late_res, res_ref), (late_jac, jac_ref))):
            for piece, start, side in ((below, starts[0], 0), (above, starts[1], 1)):
                rows = slice(side * layer, (side + 1) * layer)
                value = late_ref[coef - late, :, rows]
                if coef >= start:
                    value = value - piece[field, coef - start]
                stage[field, coef - first, :, rows] = value
            copy = pltpu.make_async_copy(
                stage.at[field, coef - first], out_ref.at[coef], sems.at[field, coef - first]
            )
            copy.start()
            copies.append(copy)
    for copy in copies:
        copy.wait()


def transform_table(time_count, coef_count):
    sample = np.arange(time_count)[:, None]
    coef = np.arange(coef_count)[None, :]
    angles = ((coef // 2 + 1) * sample % time_count) * (2.0 * math.pi / time_count)
    return np.where(coef % 2 == 0, np.cos(angles), np.sin(angles)).astype(np.float32)


SMALL = pl.CostEstimate(flops=1000, transcendentals=0, bytes_accessed=1000)
LARGE = pl.CostEstimate(flops=10**12, transcendentals=10**9, bytes_accessed=10**10)


def params(*semantics):
    return pltpu.CompilerParams(vmem_limit_bytes=VMEM, dimension_semantics=semantics or None)


def on_device(
    displacement,
    direction,
    forcing,
    stiffness,
    lumped_mass,
    face_cells,
    send_rows,
    pair_rows,
    status,
    crack_gap,
):
    coefs, comps, layers, radial, axial = displacement.shape
    rows = layers * radial
    slots = face_cells.shape[0]
    pairs = pair_rows.shape[1]
    owners = lax.axis_size("mesh")
    cap = slots // owners
    direct = cap % LANES == 0
    harm_count = lax.axis_size("harm")
    harm_index = lax.axis_index("harm")
    coef_total = coefs * harm_count
    place = jnp.reshape(harm_index, (1,)).astype(jnp.int32)
    f32 = jnp.float32
    values = 2 * comps * coefs
    wire = (owners, 6, coefs, cap) if direct else (6, coefs, slots)

    forward = [(i, (i + 1) % owners) for i in range(owners)]
    backward = [(target, source) for source, target in forward]
    ahead = lambda piece: lax.ppermute(piece, "mesh", forward)
    behind = lambda piece: lax.ppermute(piece, "mesh", backward)
    keep = lambda value: pltpu.with_memory_space_constraint(value, pltpu.VMEM)
    stay = lambda value: pltpu.with_memory_space_constraint(value, pltpu.HBM)

    groups = []
    done = [0, 0]
    for ends in CUTS:
        group = []
        for side, end in enumerate(ends):
            last = end * coefs // 8
            if last > done[side]:
                group.append((radial * (1 - side), done[side], last))
                done[side] = last
        groups.append(group)
    shift = lambda edge, piece: ahead(piece) if edge[0] > 0 else behind(piece)
    pieces = [
        [
            shift(
                edge,
                jnp.stack(
                    [
                        field[edge[1] : edge[2], :, edge[0] // radial]
                        for field in (displacement, direction)
                    ]
                ),
            )
            for edge in groups[0]
        ]
    ]

    x = displacement.reshape(coefs, comps, rows, axial)
    y = direction.reshape(coefs, comps, rows, axial)
    cells = face_cells.reshape(slots // LANES, LANES)
    send = send_rows.reshape(slots // LANES, LANES)
    whole = lambda shape: pl.BlockSpec(shape, lambda *_: (0,) * len(shape))
    scalar = pl.BlockSpec(memory_space=pltpu.SMEM)
    near_memory = pl.BlockSpec(memory_space=pltpu.VMEM)
    per_comp = pl.BlockSpec((coefs, 1, rows, axial), lambda comp: (0, comp, 0, 0))

    edges = [edge for group in groups[1:] for edge in group]
    edge_shapes = [(2, last - first, comps, radial, axial) for _, first, last in edges]
    outgoing, *sent = pl.pallas_call(
        lambda *refs: gather_kernel(*refs, edges=edges),
        grid=(comps,),
        in_specs=[whole(cells.shape), whole(send.shape), per_comp, per_comp],
        out_specs=[whole(wire)]
        + [
            pl.BlockSpec(shape[:2] + (1,) + shape[3:], lambda comp: (0, 0, comp, 0, 0))
            for shape in edge_shapes
        ],
        out_shape=[pltpu.HBM(shape, f32) for shape in [wire] + edge_shapes],
        scratch_shapes=[
            pltpu.VMEM((1, slots), jnp.int32),
            pltpu.VMEM((2 * axial, slots), jnp.bfloat16),
        ],
        compiler_params=params("arbitrary"),
        cost_estimate=SMALL,
        name="face_gather",
    )(cells, send, stay(x), stay(y))

    def exchange(block):
        if not direct:
            block = block.reshape(values, owners, cap).transpose(1, 0, 2)
        block = lax.all_to_all(block, "mesh", split_axis=0, concat_axis=0, tiled=True)
        if not direct:
            block = block.transpose(1, 0, 2).reshape(wire)
        return block

    queue = []
    for group in groups[1:]:
        queue.append(sent[: len(group)])
        sent = sent[len(group) :]
    send_group = lambda index: [
        shift(edge, piece) for edge, piece in zip(groups[index], queue[index - 1])
    ]
    outgoing, queue[0] = lax.optimization_barrier((outgoing, queue[0]))
    arrival = pl.pallas_call(
        mark_kernel,
        in_specs=[pl.BlockSpec(memory_space=pl.ANY)],
        out_specs=near_memory,
        out_shape=pltpu.VMEM((8, LANES), f32),
        cost_estimate=LARGE,
        name="piece_arrived",
    )
    mark = arrival(pieces[0][-1])
    pieces.append(send_group(1))
    arrived = exchange(outgoing)
    own_opening = pl.pallas_call(
        opening_kernel,
        in_specs=[whole(pair_rows.shape), whole(status.shape), near_memory, near_memory],
        out_specs=whole((values + status.shape[0], pairs)),
        out_shape=jax.ShapeDtypeStruct((values + status.shape[0], pairs), f32),
        compiler_params=params(),
        cost_estimate=SMALL,
        name="pair_difference",
    )(pair_rows, status, keep(mark), pltpu.with_memory_space_constraint(arrived, pltpu.VMEM))
    everything = lax.all_gather(own_opening, "harm")
    table = transform_table(TIME, coef_total)
    back = ((2.0 / TIME) * table.T).reshape(harm_count, coefs, TIME)
    slot_force = pl.pallas_call(
        force_kernel,
        in_specs=[
            scalar,
            whole(pair_rows.shape),
            whole((1, pairs)),
            whole(table.shape),
            whole(back.shape),
            whole(everything.shape),
        ],
        out_specs=whole(wire),
        out_shape=jax.ShapeDtypeStruct(wire, f32),
        compiler_params=params(),
        cost_estimate=LARGE,
        name="pair_force",
    )(place, pair_rows, crack_gap.reshape(1, pairs), jnp.asarray(table), jnp.asarray(back), everything)
    returned = exchange(slot_force)
    queue[1:], _ = lax.optimization_barrier((queue[1:], slot_force))
    second_mark = arrival(pieces[1][-1])
    pieces.append(send_group(2))

    flat = jax.ShapeDtypeStruct(x.shape, f32)
    piece_spec = lambda piece: pl.BlockSpec(
        piece.shape[:2] + (1,) + piece.shape[3:], lambda comp: (0, 0, comp, 0, 0)
    )
    early = groups[0] + groups[1]
    late = min(group[1] for group in groups[2])
    late_shape = pltpu.VMEM((coefs - late, comps, rows, axial), f32)
    residual, product, late_res, late_jac = pl.pallas_call(
        lambda *refs: combine_kernel(*refs, edges=early, late=late),
        grid=(comps,),
        in_specs=[near_memory, scalar, whole(cells.shape), whole(send.shape)]
        + [near_memory]
        + [piece_spec(piece) for piece in pieces[0] + pieces[1]]
        + [whole((rows, axial))] * 2
        + [per_comp] * 3,
        out_specs=[per_comp] * 2 + [near_memory] * 2,
        out_shape=[flat, flat, late_shape, late_shape],
        scratch_shapes=[
            pltpu.VMEM((1, slots), jnp.int32),
            pltpu.VMEM((axial, slots), jnp.bfloat16),
        ],
        compiler_params=params("arbitrary"),
        cost_estimate=SMALL,
        name="combine_terms",
    )(
        keep(second_mark),
        place,
        cells,
        send,
        keep(returned),
        *pieces[0],
        *pieces[1],
        stiffness.reshape(rows, axial),
        lumped_mass.reshape(rows, axial),
        stay(x),
        stay(y),
        stay(forcing.reshape(x.shape)),
    )
    residual, queue[2] = lax.optimization_barrier((residual, queue[2]))
    pieces.append(send_group(3))

    for group, piece in zip(groups[2:], pieces[2:]):
        starts = [edge[1] for edge in group]
        last = group[0][2]
        residual, product = pl.pallas_call(
            lambda *refs, starts=starts: edge_kernel(*refs, late=late, starts=starts),
            in_specs=[near_memory] * 4 + [pl.BlockSpec(memory_space=pl.ANY)] * 2,
            out_specs=[pl.BlockSpec(memory_space=pl.ANY)] * 2,
            out_shape=[flat, flat],
            input_output_aliases={4: 0, 5: 1},
            scratch_shapes=[
                pltpu.VMEM((2, last - min(starts), comps, rows, axial), f32),
                pltpu.SemaphoreType.DMA((2, last - min(starts))),
            ],
            compiler_params=params(),
            cost_estimate=LARGE if last < coefs else SMALL,
            name="edge_terms",
        )(keep(late_res), keep(late_jac), *[keep(value) for value in piece], residual, product)
    return residual.reshape(displacement.shape), product.reshape(displacement.shape)


def solution(mesh):
    placed = (
        P("harm", None, "mesh", None, None),
        P("harm", None, "mesh", None, None),
        P("harm", None, "mesh", None, None),
        P("mesh", None, None),
        P("mesh", None, None),
        P("mesh"),
        P("mesh"),
        P(None, "mesh"),
        P("harm", "mesh"),
        P("mesh"),
    )
    return jax.shard_map(
        on_device,
        mesh=mesh,
        in_specs=placed,
        out_specs=(P("harm", None, "mesh", None, None), P("harm", None, "mesh", None, None)),
        check_vma=False,
    )
```

```python
import math

import jax
import jax.numpy as jnp
import numpy as np
from jax import lax
from jax.experimental import pallas as pl
from jax.experimental.pallas import tpu as pltpu
from jax.sharding import PartitionSpec as P

HARM = 16
TIME = 64
LANES = 128

damping_ratio = 0.3
normal_penalty = 2.0
shear_penalty = 1.0

CUTS = ((3, 0), (3, 5), (7, 7), (8, 8))
VMEM = 20 * 1024 * 1024


def split2(value):
    high = value.astype(jnp.bfloat16)
    low = (value - high.astype(jnp.float32)).astype(jnp.bfloat16)
    return high, low


def split3(value):
    high = value.astype(jnp.bfloat16)
    rest = value - high.astype(jnp.float32)
    mid = rest.astype(jnp.bfloat16)
    low = (rest - mid.astype(jnp.float32)).astype(jnp.bfloat16)
    return high, mid, low


def slot_cells(cells_ref, send_ref):
    rows = cells_ref.shape[0]
    send = send_ref[...]
    high = send // LANES
    low = send % LANES
    found = jnp.zeros_like(send)
    for row in range(rows):
        table = jnp.broadcast_to(cells_ref[row : row + 1, :], send.shape)
        picked = jnp.take_along_axis(table, low, axis=1)
        found = jnp.where(high == row, picked, found)
    return jnp.concatenate([found[row : row + 1, :] for row in range(rows)], axis=1)


def one_hot_rows(index_row, count, kind):
    shape = (count, index_row.shape[1])
    hit = lax.broadcasted_iota(jnp.int32, shape, 0) == index_row
    return jnp.where(hit, 1.0, 0.0).astype(kind)


def gather_kernel(cells_ref, send_ref, x_ref, y_ref, out_ref, *refs, edges):
    edge_refs = refs[: len(edges)]
    cell_ref, low_ref = refs[len(edges) :]
    comp = pl.program_id(0)
    coefs, _, rows, axial = x_ref.shape
    slots = cell_ref.shape[1]

    @pl.when(comp == 0)
    def _():
        cell = slot_cells(cells_ref, send_ref)
        cell_ref[...] = cell
        hot = one_hot_rows(cell % axial, axial, jnp.bfloat16)
        low_ref[0:axial, :] = hot
        low_ref[axial : 2 * axial, :] = hot

    row_of = cell_ref[...] // axial
    mask = lax.broadcasted_iota(jnp.int32, (rows, slots), 0) == row_of
    for field, ref in enumerate((x_ref, y_ref)):
        for edge_ref, (start, first, last) in zip(edge_refs, edges):
            edge_ref[field, :, 0] = ref[first:last, 0, start : start + rows // 2]
        flat = ref[...].reshape(coefs * rows, axial)
        high, low = split2(flat)
        picked = jnp.dot(
            jnp.concatenate([high, low], axis=1),
            low_ref[...],
            preferred_element_type=jnp.float32,
        ).reshape(coefs, rows, slots)
        values = jnp.sum(jnp.where(mask[None], picked, 0.0), axis=1)
        block = field * 3 + comp
        if len(out_ref.shape) == 4:
            cap = out_ref.shape[3]
            for owner in range(out_ref.shape[0]):
                out_ref[owner, block] = values[:, owner * cap : (owner + 1) * cap]
        else:
            out_ref[block] = values


def pair_table(pairs_ref, slots):
    count = pairs_ref.shape[1]
    place = lax.broadcasted_iota(jnp.int32, (slots, count), 0)
    side_a = jnp.where(place == pairs_ref[0:1, :], 1.0, 0.0)
    side_b = jnp.where(place == pairs_ref[1:2, :], 1.0, 0.0)
    return (side_a - side_b).astype(jnp.bfloat16)


def by_slot(ref, block):
    if len(ref.shape) == 3:
        return ref[block]
    return jnp.concatenate([ref[owner, block] for owner in range(ref.shape[0])], axis=1)


def mark_kernel(piece_ref, out_ref):
    del piece_ref
    out_ref[...] = jnp.zeros_like(out_ref)


def opening_kernel(pairs_ref, status_ref, mark_ref, arrived_ref, out_ref):
    del mark_ref
    arrived = jnp.concatenate([by_slot(arrived_ref, block) for block in range(6)], axis=0)
    values, slots = arrived.shape
    table = pair_table(pairs_ref, slots)
    total = None
    for part in split3(arrived):
        term = jnp.dot(part, table, preferred_element_type=jnp.float32)
        total = term if total is None else total + term
    out_ref[0:values, :] = total
    out_ref[values:, :] = status_ref[...].astype(jnp.float32)


def force_kernel(place_ref, pairs_ref, gap_ref, table_ref, back_ref, all_ref, out_ref):
    harm_count, total_rows, pairs = all_ref.shape
    coefs = table_ref.shape[1] // harm_count
    values = 6 * coefs
    back = back_ref[place_ref[0]]
    closed = jnp.concatenate([all_ref[g, values:total_rows, :] for g in range(harm_count)], axis=0)
    coef_rows = []
    for block in range(6):
        spread = jnp.concatenate(
            [all_ref[g, block * coefs : (block + 1) * coefs, :] for g in range(harm_count)], axis=0
        )
        opening = jnp.dot(
            table_ref[...], spread, precision=lax.Precision.HIGHEST, preferred_element_type=jnp.float32
        )
        if block == 0:
            opening = opening + gap_ref[...]
        kappa = normal_penalty if block % 3 == 0 else shear_penalty
        force = closed * kappa * opening
        coef_rows.append(
            jnp.dot(back, force, precision=lax.Precision.HIGHEST, preferred_element_type=jnp.float32)
        )
    coef_force = jnp.concatenate(coef_rows, axis=0)
    direct = len(out_ref.shape) == 4
    slots = out_ref.shape[0] * out_ref.shape[3] if direct else out_ref.shape[2]
    table = pair_table(pairs_ref, slots)
    total = None
    for part in split3(coef_force):
        term = lax.dot_general(
            part, table, (((1,), (1,)), ((), ())), preferred_element_type=jnp.float32
        )
        total = term if total is None else total + term
    for block in range(6):
        part = total[block * coefs : (block + 1) * coefs]
        if direct:
            cap = out_ref.shape[3]
            for owner in range(out_ref.shape[0]):
                out_ref[owner, block] = part[:, owner * cap : (owner + 1) * cap]
        else:
            out_ref[block] = part


def combine_kernel(mark_ref, place_ref, cells_ref, send_ref, back_ref, *refs, edges, late):
    del mark_ref
    piece_refs = refs[: len(edges)]
    stiff_ref, mass_ref, x_ref, y_ref, forcing_ref = refs[len(edges) : len(edges) + 5]
    res_ref, jac_ref, late_res_ref, late_jac_ref, cell_ref, low_ref = refs[len(edges) + 5 :]
    comp = pl.program_id(0)
    coefs, _, rows, axial = x_ref.shape
    slots = cell_ref.shape[1]
    layer = rows // 2
    @pl.when(comp == 0)
    def _():
        cell = slot_cells(cells_ref, send_ref)
        cell_ref[...] = cell
        low_ref[...] = one_hot_rows(cell % axial, axial, jnp.bfloat16)

    row_of = cell_ref[...] // axial
    mask = lax.broadcasted_iota(jnp.int32, (rows, slots), 0) == row_of
    row = lax.broadcasted_iota(jnp.int32, (rows, axial), 0) % layer
    column = lax.broadcasted_iota(jnp.int32, (rows, axial), 1)
    mass = mass_ref[...]
    stiff = 6.0 + stiff_ref[...]
    for field, (ref, out_ref, late_ref) in enumerate(
        ((x_ref, res_ref, late_res_ref), (y_ref, jac_ref, late_jac_ref))
    ):
        force = by_slot(back_ref, field * 3 + comp)
        contact = None
        for part in split2(force):
            wide = part.astype(jnp.float32)
            spread = jnp.where(mask[None], wide[:, None, :], 0.0).astype(jnp.bfloat16)
            term = lax.dot_general(
                spread.reshape(coefs * rows, slots),
                low_ref[...],
                (((1,), (1,)), ((), ())),
                preferred_element_type=jnp.float32,
            )
            contact = term if contact is None else contact + term
        contact = contact.reshape(coefs, rows, axial)
        for coef in range(coefs):
            harmonic = place_ref[0] * (coefs // 2) + (coef // 2 + 1)
            frequency = harmonic.astype(jnp.float32) * (1.5 / HARM)
            value = ref[coef, 0]
            turned = ref[coef + 1, 0] if coef % 2 == 0 else -ref[coef - 1, 0]
            near = jnp.where(row == 0, 0.0, jnp.roll(value, 1, axis=0))
            near = near + jnp.where(row == layer - 1, 0.0, jnp.roll(value, -1, axis=0))
            near = near + jnp.where(column == 0, 0.0, pltpu.roll(value, 1, axis=1))
            near = near + jnp.where(column == axial - 1, 0.0, pltpu.roll(value, axial - 1, axis=1))
            near = near + jnp.concatenate([value[layer:], value[:layer]], axis=0)
            result = (stiff - (frequency * frequency) * mass) * value - near
            result = result + (frequency * damping_ratio) * mass * turned + contact[coef]
            if field == 0:
                result = result - forcing_ref[coef, 0]
            parts = [result[:layer], result[layer:]]
            for piece_ref, (start, first, last) in zip(piece_refs, edges):
                if first <= coef < last:
                    side = 0 if start > 0 else 1
                    parts[side] = parts[side] - piece_ref[field, coef - first, 0]
            for side in (0, 1):
                rows_of = pl.ds(side * layer, layer)
                if coef < late:
                    out_ref[coef, 0, rows_of] = parts[side]
                else:
                    late_ref[coef - late, comp, rows_of] = parts[side]


def edge_kernel(late_res, late_jac, below, above, res_in, jac_in, res_ref, jac_ref, *refs, late, starts):
    del res_in, jac_in
    stage, sems = refs
    first = min(starts)
    count = stage.shape[1]
    layer = stage.shape[3] // 2
    copies = []
    for coef in range(first, first + count):
        for field, (late_ref, out_ref) in enumerate(((late_res, res_ref), (late_jac, jac_ref))):
            for piece, start, side in ((below, starts[0], 0), (above, starts[1], 1)):
                rows = slice(side * layer, (side + 1) * layer)
                value = late_ref[coef - late, :, rows]
                if coef >= start:
                    value = value - piece[field, coef - start]
                stage[field, coef - first, :, rows] = value
            copy = pltpu.make_async_copy(
                stage.at[field, coef - first], out_ref.at[coef], sems.at[field, coef - first]
            )
            copy.start()
            copies.append(copy)
    for copy in copies:
        copy.wait()


def transform_table(time_count, coef_count):
    sample = np.arange(time_count)[:, None]
    coef = np.arange(coef_count)[None, :]
    angles = ((coef // 2 + 1) * sample % time_count) * (2.0 * math.pi / time_count)
    return np.where(coef % 2 == 0, np.cos(angles), np.sin(angles)).astype(np.float32)


SMALL = pl.CostEstimate(flops=1000, transcendentals=0, bytes_accessed=1000)
LARGE = pl.CostEstimate(flops=10**12, transcendentals=10**9, bytes_accessed=10**10)


def params(*semantics):
    return pltpu.CompilerParams(vmem_limit_bytes=VMEM, dimension_semantics=semantics or None)


def on_device(
    displacement,
    direction,
    forcing,
    stiffness,
    lumped_mass,
    face_cells,
    send_rows,
    pair_rows,
    status,
    crack_gap,
):
    coefs, comps, layers, radial, axial = displacement.shape
    rows = layers * radial
    slots = face_cells.shape[0]
    pairs = pair_rows.shape[1]
    owners = lax.axis_size("mesh")
    cap = slots // owners
    direct = cap % LANES == 0
    harm_count = lax.axis_size("harm")
    harm_index = lax.axis_index("harm")
    coef_total = coefs * harm_count
    place = jnp.reshape(harm_index, (1,)).astype(jnp.int32)
    f32 = jnp.float32
    values = 2 * comps * coefs
    wire = (owners, 6, coefs, cap) if direct else (6, coefs, slots)

    forward = [(i, (i + 1) % owners) for i in range(owners)]
    backward = [(target, source) for source, target in forward]
    ahead = lambda piece: lax.ppermute(piece, "mesh", forward)
    behind = lambda piece: lax.ppermute(piece, "mesh", backward)
    keep = lambda value: pltpu.with_memory_space_constraint(value, pltpu.VMEM)
    stay = lambda value: pltpu.with_memory_space_constraint(value, pltpu.HBM)

    groups = []
    done = [0, 0]
    for ends in CUTS:
        group = []
        for side, end in enumerate(ends):
            last = end * coefs // 8
            if last > done[side]:
                group.append((radial * (1 - side), done[side], last))
                done[side] = last
        groups.append(group)
    shift = lambda edge, piece: ahead(piece) if edge[0] > 0 else behind(piece)
    pieces = [
        [
            shift(
                edge,
                jnp.stack(
                    [
                        field[edge[1] : edge[2], :, edge[0] // radial]
                        for field in (displacement, direction)
                    ]
                ),
            )
            for edge in groups[0]
        ]
    ]

    x = displacement.reshape(coefs, comps, rows, axial)
    y = direction.reshape(coefs, comps, rows, axial)
    cells = face_cells.reshape(slots // LANES, LANES)
    send = send_rows.reshape(slots // LANES, LANES)
    whole = lambda shape: pl.BlockSpec(shape, lambda *_: (0,) * len(shape))
    scalar = pl.BlockSpec(memory_space=pltpu.SMEM)
    near_memory = pl.BlockSpec(memory_space=pltpu.VMEM)
    per_comp = pl.BlockSpec((coefs, 1, rows, axial), lambda comp: (0, comp, 0, 0))

    edges = [edge for group in groups[1:] for edge in group]
    edge_shapes = [(2, last - first, comps, radial, axial) for _, first, last in edges]
    outgoing, *sent = pl.pallas_call(
        lambda *refs: gather_kernel(*refs, edges=edges),
        grid=(comps,),
        in_specs=[whole(cells.shape), whole(send.shape), per_comp, per_comp],
        out_specs=[whole(wire)]
        + [
            pl.BlockSpec(shape[:2] + (1,) + shape[3:], lambda comp: (0, 0, comp, 0, 0))
            for shape in edge_shapes
        ],
        out_shape=[pltpu.HBM(shape, f32) for shape in [wire] + edge_shapes],
        scratch_shapes=[
            pltpu.VMEM((1, slots), jnp.int32),
            pltpu.VMEM((2 * axial, slots), jnp.bfloat16),
        ],
        compiler_params=params("arbitrary"),
        cost_estimate=SMALL,
        name="face_gather",
    )(cells, send, stay(x), stay(y))

    def exchange(block):
        if not direct:
            block = block.reshape(values, owners, cap).transpose(1, 0, 2)
        block = lax.all_to_all(block, "mesh", split_axis=0, concat_axis=0, tiled=True)
        if not direct:
            block = block.transpose(1, 0, 2).reshape(wire)
        return block

    queue = []
    for group in groups[1:]:
        queue.append(sent[: len(group)])
        sent = sent[len(group) :]
    send_group = lambda index: [
        shift(edge, piece) for edge, piece in zip(groups[index], queue[index - 1])
    ]
    outgoing, queue[0] = lax.optimization_barrier((outgoing, queue[0]))
    arrival = pl.pallas_call(
        mark_kernel,
        in_specs=[pl.BlockSpec(memory_space=pl.ANY)],
        out_specs=near_memory,
        out_shape=pltpu.VMEM((8, LANES), f32),
        cost_estimate=LARGE,
        name="piece_arrived",
    )
    mark = arrival(pieces[0][-1])
    pieces.append(send_group(1))
    arrived = exchange(outgoing)
    own_opening = pl.pallas_call(
        opening_kernel,
        in_specs=[whole(pair_rows.shape), whole(status.shape), near_memory, near_memory],
        out_specs=whole((values + status.shape[0], pairs)),
        out_shape=jax.ShapeDtypeStruct((values + status.shape[0], pairs), f32),
        compiler_params=params(),
        cost_estimate=SMALL,
        name="pair_difference",
    )(pair_rows, status, keep(mark), pltpu.with_memory_space_constraint(arrived, pltpu.VMEM))
    everything = lax.all_gather(own_opening, "harm")
    table = transform_table(TIME, coef_total)
    back = ((2.0 / TIME) * table.T).reshape(harm_count, coefs, TIME)
    slot_force = pl.pallas_call(
        force_kernel,
        in_specs=[
            scalar,
            whole(pair_rows.shape),
            whole((1, pairs)),
            whole(table.shape),
            whole(back.shape),
            whole(everything.shape),
        ],
        out_specs=whole(wire),
        out_shape=jax.ShapeDtypeStruct(wire, f32),
        compiler_params=params(),
        cost_estimate=LARGE,
        name="pair_force",
    )(place, pair_rows, crack_gap.reshape(1, pairs), jnp.asarray(table), jnp.asarray(back), everything)
    returned = exchange(slot_force)
    queue[1:], _ = lax.optimization_barrier((queue[1:], slot_force))
    second_mark = arrival(pieces[1][-1])
    pieces.append(send_group(2))

    flat = jax.ShapeDtypeStruct(x.shape, f32)
    piece_spec = lambda piece: pl.BlockSpec(
        piece.shape[:2] + (1,) + piece.shape[3:], lambda comp: (0, 0, comp, 0, 0)
    )
    early = groups[0] + groups[1]
    late = min(group[1] for group in groups[2])
    late_shape = pltpu.VMEM((coefs - late, comps, rows, axial), f32)
    residual, product, late_res, late_jac = pl.pallas_call(
        lambda *refs: combine_kernel(*refs, edges=early, late=late),
        grid=(comps,),
        in_specs=[near_memory, scalar, whole(cells.shape), whole(send.shape)]
        + [near_memory]
        + [piece_spec(piece) for piece in pieces[0] + pieces[1]]
        + [whole((rows, axial))] * 2
        + [per_comp] * 3,
        out_specs=[per_comp] * 2 + [near_memory] * 2,
        out_shape=[flat, flat, late_shape, late_shape],
        scratch_shapes=[
            pltpu.VMEM((1, slots), jnp.int32),
            pltpu.VMEM((axial, slots), jnp.bfloat16),
        ],
        compiler_params=params("arbitrary"),
        cost_estimate=SMALL,
        name="combine_terms",
    )(
        keep(second_mark),
        place,
        cells,
        send,
        keep(returned),
        *pieces[0],
        *pieces[1],
        stiffness.reshape(rows, axial),
        lumped_mass.reshape(rows, axial),
        stay(x),
        stay(y),
        stay(forcing.reshape(x.shape)),
    )
    residual, queue[2] = lax.optimization_barrier((residual, queue[2]))
    pieces.append(send_group(3))

    for group, piece in zip(groups[2:], pieces[2:]):
        starts = [edge[1] for edge in group]
        last = group[0][2]
        residual, product = pl.pallas_call(
            lambda *refs, starts=starts: edge_kernel(*refs, late=late, starts=starts),
            in_specs=[near_memory] * 4 + [pl.BlockSpec(memory_space=pl.ANY)] * 2,
            out_specs=[pl.BlockSpec(memory_space=pl.ANY)] * 2,
            out_shape=[flat, flat],
            input_output_aliases={4: 0, 5: 1},
            scratch_shapes=[
                pltpu.VMEM((2, last - min(starts), comps, rows, axial), f32),
                pltpu.SemaphoreType.DMA((2, last - min(starts))),
            ],
            compiler_params=params(),
            cost_estimate=LARGE if last < coefs else SMALL,
            name="edge_terms",
        )(keep(late_res), keep(late_jac), *[keep(value) for value in piece], residual, product)
    return residual.reshape(displacement.shape), product.reshape(displacement.shape)


def solution(mesh):
    placed = (
        P("harm", None, "mesh", None, None),
        P("harm", None, "mesh", None, None),
        P("harm", None, "mesh", None, None),
        P("mesh", None, None),
        P("mesh", None, None),
        P("mesh"),
        P("mesh"),
        P(None, "mesh"),
        P("harm", "mesh"),
        P("mesh"),
    )
    return jax.shard_map(
        on_device,
        mesh=mesh,
        in_specs=placed,
        out_specs=(P("harm", None, "mesh", None, None), P("harm", None, "mesh", None, None)),
        check_vma=False,
    )
```
